32 devices in a mesh: survey: 2 (over x), freq: 16 (over z, y, core).
Axes of the slice: x: 2, y: 2, z: 4, core: 2. Of those that a mesh axis runs over, the one named last changes fastest.
Arguments:
- gathers: float32 [4096, 2048], P(('survey', 'freq')), parts along dimension 0, may hold values from -6 to 6
- operator: bfloat16 [64, 2, 1024, 1024], P(('survey', 'freq')), parts along dimension 0, may hold values from -0.125 to 0.125
- filters: float32 [32, 4, 9, 31], P(('survey', 'freq')), parts along dimension 0, may hold values from -0.18 to 0.18
- tile_of: int32 [32], P('survey'), parts along dimension 0, may hold values from 0 to 15, each once
- slice_len: int32 [32], P('survey'), parts along dimension 0, may hold values from 1 to 2, 20 in all
Outputs:
- primaries: float32 [4096, 2048], P(('survey', 'freq')), parts along dimension 0
The draws below stay inside these ranges and needn't reach their ends.
There are 2 independent parts, one for each index of `survey`. The reference program is written for one: setup_inputs(seed, part) draws one part's arguments, and reference() takes and returns one part's arrays. A program takes and returns all parts, laid end to end along the dimension named above; each array names one. Nothing has to cross between parts.
Inputs may be any that keep to these rules, and one draw needn't show every extreme that they name: `tile_of`: each tile is held by exactly one block of rows. `slice_len`: the entries sum to 20; the largest equals 2.
All inputs are finite; a program needn't handle non-finite values.
Results may differ from the reference program's by a relative error of at most 0.0027.
Values may be sent and summed in bfloat16 or wider, within the bound.
A program may use at most 64 MiB of HBM per device.

```python
import math
import jax
import jax.numpy as jnp
import numpy as np
from jax import lax

R = 1024
NT = 2048
TRACES_DEV = 128
MOST = 2
FIRST = 40
SHOTS = 2
BAND = 32
KEPT = 20
N_FREQ = 16


def block_levels(own_key, dims, cuts, least, high):
    gain, own = 1.0, jax.random.fold_in(own_key, 6)
    for dim, shards_of in cuts:
        steps = jnp.exp(jax.random.uniform(jax.random.fold_in(own, dim), (shards_of,), jnp.float32, least / len(cuts), high / len(cuts)))
        gain = gain * jnp.repeat(steps, dims[dim] // shards_of).reshape([-1 if axis == dim else 1 for axis in range(len(dims))])
    return gain


def split_up(amount, total, most, skew):
    loads = [(1 << 20) // math.isqrt(rank ** skew) + 1 for rank in range(2, amount + 1)]
    spare, counts = total - most - (amount - 1), [1] * (amount - 1)
    while spare > 0:
        free = [i for i in range(amount - 1) if counts[i] < most]
        pool, remaining = sum([loads[i] for i in free]), spare
        for i in free:
            extra = min(most - counts[i], max(1, remaining * loads[i] // pool), spare)
            counts[i] = counts[i] + extra
            spare = spare - extra
    return np.array([most] + counts)


def uneven(rng, amount, total, reach, lean):
    if amount == 2:
        one = jax.random.randint(rng, (), max(1, total - reach), min(reach, total - 1) + 1)
        return jnp.stack([one, total - one])
    tallies = jnp.asarray(split_up(amount, total, reach, lean), jnp.int32)
    pairs = (amount - 1) // 2
    source_of, receiver = tallies[1:1 + 2 * pairs:2], tallies[2:2 + 2 * pairs:2]
    room = jnp.minimum(source_of - 1, reach - receiver)
    passed = jax.random.randint(jax.random.fold_in(rng, 1), (pairs,), 0, 1 << 20) % (room + 1)
    tallies = tallies.at[1:1 + 2 * pairs:2].set(source_of - passed).at[2:2 + 2 * pairs:2].set(receiver + passed)
    return tallies[jax.random.permutation(jax.random.fold_in(rng, 2), amount)]


def scatter_about(own_key, shape, width, bound, split=(), kind=jnp.bfloat16):
    factor_of = block_levels(own_key, shape, split, -0.22, 0.18) if split else 1.0
    drawn = jax.random.normal(own_key, shape, jnp.float32) * width * factor_of
    return jnp.minimum(jnp.maximum(drawn, -bound), bound).astype(kind)


def setup_inputs(seed: int = 0, part: int = 0) -> dict:
    keys = jax.random.split(jax.random.key(seed), 6)
    part_keys = jax.random.split(jax.random.fold_in(keys[5], part), 6)
    return {
        "gathers": scatter_about(part_keys[0], (N_FREQ * TRACES_DEV, NT), 1.0, 6.0, ((0, 16),), jnp.float32),
        "operator": scatter_about(part_keys[1], (BAND, 2, R, R), (2 * R) ** -0.5, 0.125, ((0, 16),)),
        "filters": scatter_about(part_keys[2], (N_FREQ, 4, 9, 31), 0.03, 0.18, ((0, 16),), jnp.float32),
        "tile_of": jax.random.permutation(part_keys[3], N_FREQ).astype(jnp.int32),
        "slice_len": uneven(part_keys[4], N_FREQ, KEPT, MOST, 2).astype(jnp.int32),
    }


def band_tables(first_bin, band_bins, length):
    bin_ids = first_bin + jnp.arange(band_bins, dtype=jnp.int32)
    time_ids = jnp.arange(length, dtype=jnp.int32)
    phase_ids = bin_ids[:, None] * time_ids[None, :] % length
    angles = 2.0 * math.pi / length * phase_ids.astype(jnp.float32)
    return (jnp.cos(angles), jnp.sin(angles))

def forward_table(first_bin, band_bins, length):
    cosine_rows, sine_rows = band_tables(first_bin, band_bins, length)
    return jnp.concatenate([cosine_rows, -sine_rows], axis=0) * (1.0 / math.sqrt(length))

def band_mask(slice_len, band_bins, slot_count):
    bin_ids = jnp.arange(band_bins, dtype=jnp.int32)
    device_ids = jnp.arange(slice_len.shape[0], dtype=jnp.int32)
    group_ids = bin_ids // slot_count
    kept_count = lax.optimization_barrier(jnp.sum(jnp.where(group_ids[:, None] == device_ids[None, :], slice_len[None, :], 0), axis=1))
    return (bin_ids % slot_count < kept_count).astype(jnp.float32)

def match_response(band_rows, kept, filters, first_bin, length, kept_bins):
    band_bins = band_rows.shape[0]
    traces = band_rows.shape[2] - 8
    bin_ids = first_bin + jnp.arange(band_bins, dtype=jnp.int32)
    lag_ids = jnp.arange(31, dtype=jnp.int32) - 15
    phase_ids = bin_ids[:, None] * lag_ids[None, :] % length
    angles = 2.0 * math.pi / length * phase_ids.astype(jnp.float32)
    h_real = jnp.einsum('cab,fb->caf', filters, jnp.cos(angles), precision=lax.Precision.HIGHEST)
    h_imag = jnp.einsum('cab,fb->caf', filters, jnp.sin(angles), precision=lax.Precision.HIGHEST)
    weight = bin_ids.astype(jnp.float32) / (first_bin + band_bins)
    k_real = h_real[0] + h_imag[1] - weight * h_imag[2] + weight * h_real[3]
    k_imag = h_imag[0] - h_real[1] + weight * h_real[2] + weight * h_imag[3]
    rows = band_rows.astype(jnp.float32)
    s_real = jnp.zeros((band_bins, traces), jnp.float32)
    s_imag = jnp.zeros((band_bins, traces), jnp.float32)
    for offset in range(9):
        real_rows = rows[:, 0, offset:offset + traces]
        imag_rows = rows[:, 1, offset:offset + traces]
        s_real = s_real + k_real[offset][:, None] * real_rows - k_imag[offset][:, None] * imag_rows
        s_imag = s_imag + k_real[offset][:, None] * imag_rows + k_imag[offset][:, None] * real_rows
    scale = (math.sqrt(2.0 / kept_bins) * kept)[:, None]
    stacked = jnp.concatenate([s_real * scale, s_imag * scale], axis=0)
    cosine_rows, sine_rows = band_tables(first_bin, band_bins, length)
    table = jnp.concatenate([cosine_rows, -sine_rows], axis=0)
    return lax.dot_general(stacked, table, (((0,), (0,)), ((), ())), precision=lax.Precision.HIGHEST, preferred_element_type=jnp.float32)

def predict(pair):
    spec_plane, operator_pair = pair
    contract = (((1,), (1,)), ((), ()))

    def multiply(left, right):
        return lax.dot_general(left, right, contract, preferred_element_type=jnp.float32)
    real_part = multiply(spec_plane[0], operator_pair[0]) - multiply(spec_plane[1], operator_pair[1])
    imag_part = multiply(spec_plane[0], operator_pair[1]) + multiply(spec_plane[1], operator_pair[0])
    return jnp.stack([real_part, imag_part]).astype(jnp.bfloat16)

def reference(gathers, operator, filters, tile_of, slice_len):
    per_shot = R // TRACES_DEV
    holder = jnp.argsort(tile_of).astype(jnp.int32)
    blocks = gathers.reshape(N_FREQ, TRACES_DEV, NT)
    ordered = jnp.take(blocks, holder, axis=0).reshape(SHOTS * R, NT)
    spectrum = lax.dot_general(forward_table(FIRST, BAND, NT), ordered, (((1,), (1,)), ((), ())), precision=lax.Precision.HIGHEST, preferred_element_type=jnp.float32)
    spectrum = spectrum.astype(jnp.bfloat16).reshape(2, BAND, SHOTS, R)
    predicted = lax.map(predict, (jnp.moveaxis(spectrum, 1, 0), operator))
    widened = jnp.pad(predicted, ((0, 0), (0, 0), (0, 0), (4, 4)))
    kept = band_mask(slice_len, BAND, MOST)

    def cleaned(device_index):
        tile_index = tile_of[device_index]
        shot_index = tile_index // per_shot
        start_index = tile_index % per_shot * TRACES_DEV
        anchor = jnp.zeros((), jnp.int32)
        piece = lax.dynamic_slice(widened, (anchor, anchor, shot_index, start_index), (BAND, 2, 1, TRACES_DEV + 8))[:, :, 0]
        response = match_response(piece, kept, filters[device_index], FIRST, NT, KEPT)
        return blocks[device_index] - response
    result = lax.map(cleaned, jnp.arange(N_FREQ, dtype=jnp.int32))
    return result.reshape(N_FREQ * TRACES_DEV, NT)
```

```python
import functools
import math

import jax
import jax.numpy as jnp
import numpy as np
from jax import lax
from jax.experimental import pallas as pl
from jax.experimental.pallas import tpu as pltpu
from jax.sharding import PartitionSpec as P

FIRST = 40
TAPS = 9
HALO = 4
LAGS = 31
MESH = pl.DeviceIdType.MESH


def row_bins(devices, slots):
    row = np.arange(devices * 2 * slots)
    return row // (2 * slots) * slots + row % slots, row // slots % 2


def wave_table(devices, slots, length):
    bins, part = row_bins(devices, slots)
    phase = (FIRST + bins)[:, None] * np.arange(length)[None, :] % length
    angle = 2.0 * math.pi / length * phase
    table = np.where(part[:, None] == 0, np.cos(angle), -np.sin(angle)).astype(np.float32)
    high = table.astype(jnp.bfloat16)
    low = (table - high.astype(np.float32)).astype(jnp.bfloat16)
    return np.concatenate([high, low], axis=0)


def lag_table(devices, slots, length, kept_bins):
    bins, part = row_bins(devices, slots)
    freq = FIRST + bins
    phase = freq[:, None] * (np.arange(LAGS) - LAGS // 2)[None, :] % length
    angle = 2.0 * math.pi / length * phase
    cosine, sine = np.cos(angle), np.sin(angle)
    weight = (freq / (FIRST + devices * slots))[:, None]
    real = np.stack([cosine, sine, -weight * sine, weight * cosine])
    imag = np.stack([sine, -cosine, weight * cosine, weight * sine])
    imag = np.where(part[None, :, None] == 0, imag, -imag)
    scale = math.sqrt(2.0 / kept_bins)
    return (np.concatenate([real, imag], axis=1) * scale).astype(np.float32)


def step(
    n, slots, gathers, operator, filters_hbm, tile_hbm, len_hbm, waves, lags_hbm, out,
    g_buf, op_bufs, t_buf, send1, recv1, x_buf, a_buf, a_pred, pieces, send2, recv2,
    z_buf, k_buf, holder, place, order, filters, lags, tile_of, slice_len,
    g_sem, op_sem, t_sem, small_sem, own_sem, s1, r1, s2, r2,
):
    me = lax.axis_index("freq")
    traces, length = g_buf.shape
    receivers = op_bufs[0].shape[1]
    width = 2 * slots
    rows = n * width
    per_shot = receivers // traces
    shots = n // per_shot
    turn = shots * width

    upper = me // (n // 2)

    def seat(i):
        return upper * (n - 1 - i) + (1 - upper) * i

    def far(i):
        at = n - 1 - i
        at = at - (n - at + seat(me)) // n
        return seat(at)

    barrier = pltpu.get_barrier_semaphore()

    def greet(i, carry):
        pl.semaphore_signal(
            barrier, inc=1, device_id={"freq": far(i)}, device_id_type=MESH
        )
        return carry

    lax.fori_loop(0, n - 1, greet, 0, unroll=n <= 16)

    g_copy = pltpu.make_async_copy(gathers, g_buf, g_sem)
    g_copy.start()
    t_copy = pltpu.make_async_copy(waves, t_buf.at[pl.ds(0, 2 * rows)], t_sem.at[0])
    t_copy.start()
    small_copies = []
    for i, (src, dst) in enumerate(
        ((filters_hbm, filters), (lags_hbm, lags), (tile_hbm, tile_of), (len_hbm, slice_len))
    ):
        copy = pltpu.make_async_copy(src, dst, small_sem.at[i])
        copy.start()
        small_copies.append(copy)
    g_copy.wait()
    for m in range(slots):
        for d in range(2):
            for q in range(per_shot):
                pltpu.make_async_copy(
                    operator.at[m, d, :, pl.ds(q * traces, traces)],
                    op_bufs[2 * m + d].at[q], op_sem.at[2 * m + d],
                ).start()
    u_copy = pltpu.make_async_copy(
        waves.at[pl.ds(0, rows)], t_buf.at[pl.ds(2 * rows, rows)], t_sem.at[1]
    )
    u_copy.start()

    data = g_buf[...]
    high = data.astype(jnp.bfloat16)
    low = (data - high.astype(jnp.float32)).astype(jnp.bfloat16)
    t_copy.wait()
    product = lax.dot_general(
        t_buf[0 : 2 * rows], high, (((1,), (1,)), ((), ())),
        preferred_element_type=jnp.float32,
    )
    rest = lax.dot_general(
        t_buf[0:rows], low, (((1,), (1,)), ((), ())), preferred_element_type=jnp.float32
    )
    spectrum = (product[0:rows] + product[rows : 2 * rows] + rest) * (1.0 / math.sqrt(length))
    spectrum = spectrum.astype(jnp.bfloat16)
    for d in range(n):
        send1[d] = spectrum[d * width : (d + 1) * width]

    def copy1(other):
        return pltpu.make_async_remote_copy(
            src_ref=send1.at[other], dst_ref=recv1.at[me],
            send_sem=s1, recv_sem=r1.at[me],
            device_id={"freq": other}, device_id_type=MESH,
        )

    def copy2(other):
        return pltpu.make_async_remote_copy(
            src_ref=send2.at[other], dst_ref=recv2.at[me],
            send_sem=s2, recv_sem=r2,
            device_id={"freq": other}, device_id_type=MESH,
        )

    pl.semaphore_wait(barrier, n - 1)

    def start1(i, carry):
        copy1(far(i)).start()
        return carry

    lax.fori_loop(0, n - 1, start1, 0, unroll=n <= 16)
    own1 = pltpu.make_async_copy(send1.at[me], recv1.at[me], r1.at[me])
    own1.start()

    for copy in small_copies:
        copy.wait()

    def find(t, carry):
        at = jnp.int32(0)
        for k in range(n):
            at = jnp.where(tile_of[k] == t, k, at)
        holder[t] = at
        return carry

    lax.fori_loop(0, n, find, 0)
    spots = [holder[i] for i in range(n)]
    ends = []
    for q in range(per_shot):
        last = seat(spots[q])
        for s in range(1, shots):
            late = seat(spots[s * per_shot + q])
            last = jnp.where(late > last, late, last)
        ends.append(last)
    ranks = [
        sum([jnp.where(other < end, 1, 0) for other in ends], jnp.int32(0)) for end in ends
    ]
    for j in range(per_shot):
        at = jnp.int32(0)
        picks = [jnp.int32(0)] * shots
        for q, rank in enumerate(ranks):
            at = jnp.where(rank == j, q, at)
            picks = [
                jnp.where(rank == j, spots[s * per_shot + q], pick)
                for s, pick in enumerate(picks)
            ]
        order[j] = at
        for s, pick in enumerate(picks):
            place[s * per_shot + j] = pick

    response = jnp.zeros((2 * rows, TAPS), jnp.float32)
    for c in range(4):
        response = response + lax.dot_general(
            lags[c], filters[0, :, c, :], (((1,), (1,)), ((), ())),
            precision=lax.Precision.HIGHEST, preferred_element_type=jnp.float32,
        )
    for a in range(TAPS):
        k_buf[a] = jnp.broadcast_to(response[:, a : a + 1], (2 * rows, traces))
    x_buf[...] = jnp.zeros_like(x_buf)

    def take(i, carry):
        src = seat(i)
        pltpu.make_async_copy(send1.at[src], recv1.at[src], r1.at[src]).wait()
        x_buf[src] = recv1[src].astype(jnp.float32)
        return carry

    first = n - per_shot
    lax.fori_loop(0, first, take, 0, unroll=n <= 16)
    row = lax.broadcasted_iota(jnp.int32, (turn, traces), 0)
    is_real = row // slots % 2 == 0
    for i, op_buf in enumerate(op_bufs):
        pltpu.make_async_copy(op_buf, op_buf, op_sem.at[i]).wait()
    a_pred[...] = jnp.zeros_like(a_pred)

    def block(j, carry):
        take(first + j, 0)
        q = order[j]
        for s in range(shots):
            a_buf[j, s * width : (s + 1) * width] = x_buf[place[s * per_shot + j]]
        plain = a_buf[j]
        turned = jnp.where(
            is_real, -pltpu.roll(plain, turn - slots, axis=0), pltpu.roll(plain, slots, axis=0)
        )
        predicted = a_pred[...]
        for m in range(slots):
            for d in range(2):
                left = jnp.where(row % slots == m, turned if d else plain, 0.0)
                predicted = predicted + lax.dot_general(
                    left.astype(jnp.bfloat16), op_bufs[2 * m + d][q],
                    (((1,), (1,)), ((), ())), preferred_element_type=jnp.float32,
                )
        a_pred[...] = predicted
        return carry

    lax.fori_loop(0, per_shot, block, 0)
    predicted = a_pred[...]
    row = lax.broadcasted_iota(jnp.int32, (turn, receivers), 0)
    predicted = jnp.where(row % slots < slice_len[me], predicted, 0.0)
    shifted = pltpu.roll(
        jnp.concatenate([predicted, jnp.zeros((turn, traces), jnp.float32)], axis=1), HALO, axis=1
    ).astype(jnp.bfloat16)
    for t in range(n):
        s, q = t // per_shot, t % per_shot
        pieces[t] = shifted[s * width : (s + 1) * width, q * traces : (q + 2) * traces]
    for k in range(n):
        send2[k] = pieces[tile_of[k]]

    def start2(i, carry):
        copy2(far(i)).start()
        return carry

    lax.fori_loop(0, n - 1, start2, 0, unroll=n <= 16)
    own2 = pltpu.make_async_copy(send2.at[me], recv2.at[me], own_sem)
    own2.start()
    u_copy.wait()
    others = pl.ds(0, n - 1)
    pltpu.make_async_copy(send1.at[others], send1.at[others], s1).wait()
    own2.wait()
    pltpu.make_async_copy(recv2.at[others], recv2.at[others], r2).wait()
    for d in range(n):
        z_buf[d * width : (d + 1) * width] = recv2[d].astype(jnp.float32)
    z = z_buf[...]
    direct = jnp.zeros((rows, traces), jnp.float32)
    cross = jnp.zeros((rows, traces), jnp.float32)
    for a in range(TAPS):
        moved = (pltpu.roll(z, 2 * traces - a, axis=1) if a else z)[:, 0:traces]
        direct = direct + k_buf[a, 0:rows] * moved
        cross = cross + k_buf[a, rows : 2 * rows] * moved
    row = lax.broadcasted_iota(jnp.int32, cross.shape, 0)
    matched = direct + jnp.where(
        row // slots % 2 == 0,
        pltpu.roll(cross, rows - slots, axis=0),
        pltpu.roll(cross, slots, axis=0),
    )
    matched = matched.T
    high = matched.astype(jnp.bfloat16)
    low = (matched - high.astype(jnp.float32)).astype(jnp.bfloat16)
    left = jnp.concatenate([high, high, low], axis=1)
    tile = length // 4
    for j in range(4):
        span = pl.ds(j * tile, tile)
        out[:, span] = g_buf[:, span] - jnp.dot(
            left, t_buf[:, span], preferred_element_type=jnp.float32
        )
    pltpu.make_async_copy(send2.at[others], send2.at[others], s2).wait()


def local(gathers, operator, filters, tile_of, slice_len):
    n = lax.axis_size("freq")
    traces, length = gathers.shape
    slots, _, receivers, _ = operator.shape
    width = 2 * slots
    rows = n * width
    per_shot = receivers // traces
    turn = n // per_shot * width
    waves = jnp.asarray(wave_table(n, slots, length))
    lags = jnp.asarray(lag_table(n, slots, length, 5 * n // 4))
    hbm = pl.BlockSpec(memory_space=pltpu.HBM)
    taps = filters.transpose(0, 2, 1, 3)
    bf16, f32 = jnp.bfloat16, jnp.float32
    dma = pltpu.SemaphoreType.DMA
    return pl.pallas_call(
        functools.partial(step, n, slots),
        out_shape=jax.ShapeDtypeStruct(gathers.shape, f32),
        in_specs=[hbm] * 7,
        out_specs=pl.BlockSpec(memory_space=pltpu.VMEM),
        scratch_shapes=[
            pltpu.VMEM((traces, length), f32),
            [pltpu.VMEM((per_shot, receivers, traces), bf16)] * (2 * slots),
            pltpu.VMEM((3 * rows, length), bf16),
            pltpu.VMEM((n, width, traces), bf16),
            pltpu.VMEM((n, width, traces), bf16),
            pltpu.VMEM((n, width, traces), f32),
            pltpu.VMEM((per_shot, turn, traces), f32),
            pltpu.VMEM((turn, receivers), f32),
            pltpu.VMEM((n, width, 2 * traces), bf16),
            pltpu.VMEM((n, width, 2 * traces), bf16),
            pltpu.VMEM((n, width, 2 * traces), bf16),
            pltpu.VMEM((rows, 2 * traces), f32),
            pltpu.VMEM((TAPS, 2 * rows, traces), f32),
            pltpu.SMEM((n,), jnp.int32),
            pltpu.SMEM((n,), jnp.int32),
            pltpu.SMEM((per_shot,), jnp.int32),
            pltpu.VMEM(taps.shape, f32),
            pltpu.VMEM(lags.shape, f32),
            pltpu.SMEM(tile_of.shape, jnp.int32),
            pltpu.SMEM(slice_len.shape, jnp.int32),
            dma,
            dma((2 * slots,)),
            dma((2,)),
            dma((4,)),
            dma,
            dma,
            dma((n,)),
            dma,
            dma,
        ],
        compiler_params=pltpu.CompilerParams(
            collective_id=0, has_side_effects=True, vmem_limit_bytes=48*1024*1024
        ),
    )(*[pltpu.with_memory_space_constraint(x, pltpu.HBM) for x in (gathers, operator, taps, tile_of, slice_len, waves, lags)])


def solution(mesh):
    placed = (
        P(("survey", "freq"), None),
        P(("survey", "freq"), None, None, None),
        P(("survey", "freq"), None, None, None),
        P("survey"),
        P("survey"),
    )
    return jax.shard_map(
        local, mesh=mesh, in_specs=placed, out_specs=P(("survey", "freq"), None), check_vma=False
    )
```

```python
import functools
import math

import jax
import jax.numpy as jnp
import numpy as np
from jax import lax
from jax.experimental import pallas as pl
from jax.experimental.pallas import tpu as pltpu
from jax.sharding import PartitionSpec as P

FIRST = 40
TAPS = 9
HALO = 4
LAGS = 31
MESH = pl.DeviceIdType.MESH


def row_bins(devices, slots):
    row = np.arange(devices * 2 * slots)
    return row // (2 * slots) * slots + row % slots, row // slots % 2


def wave_table(devices, slots, length):
    bins, part = row_bins(devices, slots)
    phase = (FIRST + bins)[:, None] * np.arange(length)[None, :] % length
    angle = 2.0 * math.pi / length * phase
    table = np.where(part[:, None] == 0, np.cos(angle), -np.sin(angle)).astype(np.float32)
    high = table.astype(jnp.bfloat16)
    low = (table - high.astype(np.float32)).astype(jnp.bfloat16)
    return np.concatenate([high, low], axis=0)


def lag_table(devices, slots, length, kept_bins):
    bins, part = row_bins(devices, slots)
    freq = FIRST + bins
    phase = freq[:, None] * (np.arange(LAGS) - LAGS // 2)[None, :] % length
    angle = 2.0 * math.pi / length * phase
    cosine, sine = np.cos(angle), np.sin(angle)
    weight = (freq / (FIRST + devices * slots))[:, None]
    real = np.stack([cosine, sine, -weight * sine, weight * cosine])
    imag = np.stack([sine, -cosine, weight * cosine, weight * sine])
    imag = np.where(part[None, :, None] == 0, imag, -imag)
    scale = math.sqrt(2.0 / kept_bins)
    return (np.concatenate([real, imag], axis=1) * scale).astype(np.float32)


def step(
    n, slots, gathers, operator, filters_hbm, tile_hbm, len_hbm, waves, lags_hbm, out,
    g_buf, op_bufs, t_buf, send1, recv1, x_buf, a_buf, a_pred, pieces, send2, recv2,
    z_buf, k_buf, holder, place, order, filters, lags, tile_of, slice_len,
    g_sem, op_sem, t_sem, small_sem, own_sem, s1, r1, s2, r2,
):
    me = lax.axis_index("freq")
    traces, length = g_buf.shape
    receivers = op_bufs[0].shape[1]
    width = 2 * slots
    rows = n * width
    per_shot = receivers // traces
    shots = n // per_shot
    turn = shots * width

    upper = me // (n // 2)

    def seat(i):
        return upper * (n - 1 - i) + (1 - upper) * i

    def far(i):
        at = n - 1 - i
        at = at - (n - at + seat(me)) // n
        return seat(at)

    barrier = pltpu.get_barrier_semaphore()

    def greet(i, carry):
        pl.semaphore_signal(
            barrier, inc=1, device_id={"freq": far(i)}, device_id_type=MESH
        )
        return carry

    lax.fori_loop(0, n - 1, greet, 0, unroll=n <= 16)

    g_copy = pltpu.make_async_copy(gathers, g_buf, g_sem)
    g_copy.start()
    t_copy = pltpu.make_async_copy(waves, t_buf.at[pl.ds(0, 2 * rows)], t_sem.at[0])
    t_copy.start()
    small_copies = []
    for i, (src, dst) in enumerate(
        ((filters_hbm, filters), (lags_hbm, lags), (tile_hbm, tile_of), (len_hbm, slice_len))
    ):
        copy = pltpu.make_async_copy(src, dst, small_sem.at[i])
        copy.start()
        small_copies.append(copy)
    for m in range(slots):
        for d in range(2):
            for q in range(per_shot):
                pltpu.make_async_copy(
                    operator.at[m, d, :, pl.ds(q * traces, traces)],
                    op_bufs[2 * m + d].at[q], op_sem.at[2 * m + d],
                ).start(priority=1)
    u_copy = pltpu.make_async_copy(
        waves.at[pl.ds(0, rows)], t_buf.at[pl.ds(2 * rows, rows)], t_sem.at[1]
    )
    u_copy.start()

    g_copy.wait()
    data = g_buf[...]
    high = data.astype(jnp.bfloat16)
    low = (data - high.astype(jnp.float32)).astype(jnp.bfloat16)
    t_copy.wait()
    product = lax.dot_general(
        t_buf[0 : 2 * rows], high, (((1,), (1,)), ((), ())),
        preferred_element_type=jnp.float32,
    )
    rest = lax.dot_general(
        t_buf[0:rows], low, (((1,), (1,)), ((), ())), preferred_element_type=jnp.float32
    )
    spectrum = (product[0:rows] + product[rows : 2 * rows] + rest) * (1.0 / math.sqrt(length))
    spectrum = spectrum.astype(jnp.bfloat16)
    for d in range(n):
        send1[d] = spectrum[d * width : (d + 1) * width]

    def copy1(other):
        return pltpu.make_async_remote_copy(
            src_ref=send1.at[other], dst_ref=recv1.at[me],
            send_sem=s1, recv_sem=r1.at[me],
            device_id={"freq": other}, device_id_type=MESH,
        )

    def copy2(other):
        return pltpu.make_async_remote_copy(
            src_ref=send2.at[other], dst_ref=recv2.at[me],
            send_sem=s2, recv_sem=r2,
            device_id={"freq": other}, device_id_type=MESH,
        )

    pl.semaphore_wait(barrier, n - 1)

    def start1(i, carry):
        copy1(far(i)).start()
        return carry

    lax.fori_loop(0, n - 1, start1, 0, unroll=n <= 16)
    own1 = pltpu.make_async_copy(send1.at[me], recv1.at[me], r1.at[me])
    own1.start()

    for copy in small_copies:
        copy.wait()

    def find(t, carry):
        at = jnp.int32(0)
        for k in range(n):
            at = jnp.where(tile_of[k] == t, k, at)
        holder[t] = at
        return carry

    lax.fori_loop(0, n, find, 0)
    spots = [holder[i] for i in range(n)]
    ends = []
    for q in range(per_shot):
        last = seat(spots[q])
        for s in range(1, shots):
            late = seat(spots[s * per_shot + q])
            last = jnp.where(late > last, late, last)
        ends.append(last)
    ranks = [
        sum([jnp.where(other < end, 1, 0) for other in ends], jnp.int32(0)) for end in ends
    ]
    for j in range(per_shot):
        at = jnp.int32(0)
        picks = [jnp.int32(0)] * shots
        for q, rank in enumerate(ranks):
            at = jnp.where(rank == j, q, at)
            picks = [
                jnp.where(rank == j, spots[s * per_shot + q], pick)
                for s, pick in enumerate(picks)
            ]
        order[j] = at
        for s, pick in enumerate(picks):
            place[s * per_shot + j] = pick

    response = jnp.zeros((2 * rows, TAPS), jnp.float32)
    for c in range(4):
        response = response + lax.dot_general(
            lags[c], filters[0, :, c, :], (((1,), (1,)), ((), ())),
            precision=lax.Precision.HIGHEST, preferred_element_type=jnp.float32,
        )
    for a in range(TAPS):
        k_buf[a] = jnp.broadcast_to(response[:, a : a + 1], (2 * rows, traces))
    x_buf[...] = jnp.zeros_like(x_buf)

    def take(i, carry):
        src = seat(i)
        pltpu.make_async_copy(send1.at[src], recv1.at[src], r1.at[src]).wait()
        x_buf[src] = recv1[src].astype(jnp.float32)
        return carry

    first = n - per_shot
    lax.fori_loop(0, first, take, 0, unroll=n <= 16)
    row = lax.broadcasted_iota(jnp.int32, (turn, traces), 0)
    is_real = row // slots % 2 == 0
    for i, op_buf in enumerate(op_bufs):
        pltpu.make_async_copy(op_buf, op_buf, op_sem.at[i]).wait()
    a_pred[...] = jnp.zeros_like(a_pred)

    group = 1 + (per_shot + 1) % 2

    def block(i, carry):
        for e in range(group):
            take(first + group * i + e, 0)
        predicted = a_pred[...]
        for e in range(group):
            j = group * i + e
            for s in range(shots):
                a_buf[j, s * width : (s + 1) * width] = x_buf[place[s * per_shot + j]]
            plain = a_buf[j]
            turned = jnp.where(
                is_real, -pltpu.roll(plain, turn - slots, axis=0), pltpu.roll(plain, slots, axis=0)
            )
            lefts = [
                jnp.where(row % slots == m, turned if d else plain, 0.0).astype(jnp.bfloat16)
                for m in range(slots)
                for d in range(2)
            ]
            q = order[j]
            predicted = predicted + lax.dot_general(
                jnp.concatenate(lefts, axis=1),
                jnp.concatenate([op_buf[q] for op_buf in op_bufs], axis=1),
                (((1,), (1,)), ((), ())), preferred_element_type=jnp.float32,
            )
        a_pred[...] = predicted
        return carry

    lax.fori_loop(0, per_shot // group, block, 0)
    predicted = a_pred[...]
    row = lax.broadcasted_iota(jnp.int32, (turn, receivers), 0)
    predicted = jnp.where(row % slots < slice_len[me], predicted, 0.0)
    shifted = pltpu.roll(
        jnp.concatenate([predicted, jnp.zeros((turn, traces), jnp.float32)], axis=1), HALO, axis=1
    ).astype(jnp.bfloat16)
    for t in range(n):
        s, q = t // per_shot, t % per_shot
        pieces[t] = shifted[s * width : (s + 1) * width, q * traces : (q + 2) * traces]
    for k in range(n):
        send2[k] = pieces[tile_of[k]]

    def start2(i, carry):
        copy2(far(i)).start()
        return carry

    lax.fori_loop(0, n - 1, start2, 0, unroll=n <= 16)
    own2 = pltpu.make_async_copy(send2.at[me], recv2.at[me], own_sem)
    own2.start()
    u_copy.wait()
    others = pl.ds(0, n - 1)
    pltpu.make_async_copy(send1.at[others], send1.at[others], s1).wait()
    own2.wait()
    pltpu.make_async_copy(recv2.at[others], recv2.at[others], r2).wait()
    for d in range(n):
        z_buf[d * width : (d + 1) * width] = recv2[d].astype(jnp.float32)
    z = z_buf[...]
    direct = jnp.zeros((rows, traces), jnp.float32)
    cross = jnp.zeros((rows, traces), jnp.float32)
    for a in range(TAPS):
        moved = (pltpu.roll(z, 2 * traces - a, axis=1) if a else z)[:, 0:traces]
        direct = direct + k_buf[a, 0:rows] * moved
        cross = cross + k_buf[a, rows : 2 * rows] * moved
    row = lax.broadcasted_iota(jnp.int32, cross.shape, 0)
    matched = direct + jnp.where(
        row // slots % 2 == 0,
        pltpu.roll(cross, rows - slots, axis=0),
        pltpu.roll(cross, slots, axis=0),
    )
    matched = matched.T
    high = matched.astype(jnp.bfloat16)
    low = (matched - high.astype(jnp.float32)).astype(jnp.bfloat16)
    left = jnp.concatenate([high, high, low], axis=1)
    tile = length // 4
    for j in range(4):
        span = pl.ds(j * tile, tile)
        out[:, span] = g_buf[:, span] - jnp.dot(
            left, t_buf[:, span], preferred_element_type=jnp.float32
        )
    pltpu.make_async_copy(send2.at[others], send2.at[others], s2).wait()


def local(gathers, operator, filters, tile_of, slice_len):
    n = lax.axis_size("freq")
    traces, length = gathers.shape
    slots, _, receivers, _ = operator.shape
    width = 2 * slots
    rows = n * width
    per_shot = receivers // traces
    turn = n // per_shot * width
    waves = jnp.asarray(wave_table(n, slots, length))
    lags = jnp.asarray(lag_table(n, slots, length, 5 * n // 4))
    hbm = pl.BlockSpec(memory_space=pltpu.HBM)
    taps = filters.transpose(0, 2, 1, 3)
    bf16, f32 = jnp.bfloat16, jnp.float32
    dma = pltpu.SemaphoreType.DMA
    return pl.pallas_call(
        functools.partial(step, n, slots),
        out_shape=jax.ShapeDtypeStruct(gathers.shape, f32),
        in_specs=[hbm] * 7,
        out_specs=pl.BlockSpec(memory_space=pltpu.VMEM),
        scratch_shapes=[
            pltpu.VMEM((traces, length), f32),
            [pltpu.VMEM((per_shot, receivers, traces), bf16)] * (2 * slots),
            pltpu.VMEM((3 * rows, length), bf16),
            pltpu.VMEM((n, width, traces), bf16),
            pltpu.VMEM((n, width, traces), bf16),
            pltpu.VMEM((n, width, traces), f32),
            pltpu.VMEM((per_shot, turn, traces), f32),
            pltpu.VMEM((turn, receivers), f32),
            pltpu.VMEM((n, width, 2 * traces), bf16),
            pltpu.VMEM((n, width, 2 * traces), bf16),
            pltpu.VMEM((n, width, 2 * traces), bf16),
            pltpu.VMEM((rows, 2 * traces), f32),
            pltpu.VMEM((TAPS, 2 * rows, traces), f32),
            pltpu.SMEM((n,), jnp.int32),
            pltpu.SMEM((n,), jnp.int32),
            pltpu.SMEM((per_shot,), jnp.int32),
            pltpu.VMEM(taps.shape, f32),
            pltpu.VMEM(lags.shape, f32),
            pltpu.SMEM(tile_of.shape, jnp.int32),
            pltpu.SMEM(slice_len.shape, jnp.int32),
            dma,
            dma((2 * slots,)),
            dma((2,)),
            dma((4,)),
            dma,
            dma,
            dma((n,)),
            dma,
            dma,
        ],
        compiler_params=pltpu.CompilerParams(
            collective_id=0, has_side_effects=True, vmem_limit_bytes=48*1024*1024
        ),
    )(*[pltpu.with_memory_space_constraint(x, pltpu.HBM) for x in (gathers, operator, taps, tile_of, slice_len, waves, lags)])


def solution(mesh):
    placed = (
        P(("survey", "freq"), None),
        P(("survey", "freq"), None, None, None),
        P(("survey", "freq"), None, None, None),
        P("survey"),
        P("survey"),
    )
    return jax.shard_map(
        local, mesh=mesh, in_specs=placed, out_specs=P(("survey", "freq"), None), check_vma=False
    )
```

```python
import functools
import math

import jax
import jax.numpy as jnp
import numpy as np
from jax import lax
from jax.experimental import pallas as pl
from jax.experimental.pallas import tpu as pltpu
from jax.sharding import PartitionSpec as P

FIRST = 40
TAPS = 9
HALO = 4
LAGS = 31
MXU = 256
MESH = pl.DeviceIdType.MESH


def row_bins(devices, slots):
    row = np.arange(devices * 2 * slots)
    return row // (2 * slots) * slots + row % slots, row // slots % 2


def wave_table(devices, slots, length):
    bins, part = row_bins(devices, slots)
    phase = (FIRST + bins)[:, None] * np.arange(length)[None, :] % length
    angle = 2.0 * math.pi / length * phase
    table = np.where(part[:, None] == 0, np.cos(angle), -np.sin(angle)).astype(np.float32)
    high = table.astype(jnp.bfloat16)
    low = (table - high.astype(np.float32)).astype(jnp.bfloat16)
    return np.concatenate([high, low], axis=0)


def lag_table(devices, slots, length, kept_bins):
    bins, part = row_bins(devices, slots)
    freq = FIRST + bins
    phase = freq[:, None] * (np.arange(LAGS) - LAGS // 2)[None, :] % length
    angle = 2.0 * math.pi / length * phase
    cosine, sine = np.cos(angle), np.sin(angle)
    weight = (freq / (FIRST + devices * slots))[:, None]
    real = np.stack([cosine, sine, -weight * sine, weight * cosine])
    imag = np.stack([sine, -cosine, weight * cosine, weight * sine])
    imag = np.where(part[None, :, None] == 0, imag, -imag)
    scale = math.sqrt(2.0 / kept_bins)
    return (np.concatenate([real, imag], axis=1) * scale).astype(np.float32)


def step(
    n, slots, gathers, operator, filters_hbm, tile_hbm, len_hbm, waves, lags_hbm, out,
    g_buf, op_bufs, t_buf, p_buf, send1, recv1, x_buf, a_buf, a_pred, pieces, send2, recv2,
    z_buf, k_buf, holder, place, order, filters, lags, tile_of, slice_len,
    g_sem, op_sem, t_sem, small_sem, own_sem, s1, r1, s2, r2,
):
    me = lax.axis_index("freq")
    traces, length = g_buf.shape
    receivers = op_bufs[0].shape[1]
    width = 2 * slots
    rows = n * width
    per_shot = receivers // traces
    shots = n // per_shot
    turn = shots * width
    depth = t_buf.shape[0]

    upper = me // (n // 2)
    reach = upper * (n - 1 - me) + (1 - upper) * me

    def seat(i):
        inside = (2 * reach - i + n) // n
        close = me + (1 - 2 * (i % 2)) * ((i + 1) // 2)
        return inside * close + (1 - inside) * (upper * (n - 1 - i) + (1 - upper) * i)

    def rank_of(k):
        ahead = k - me
        close = jnp.where(ahead > 0, 2 * ahead, jnp.where(ahead < 0, -2 * ahead - 1, 0))
        return jnp.where(close > 2 * reach, upper * (n - 1 - k) + (1 - upper) * k, close)

    def far(i):
        return seat(n - 1 - i)

    barrier = pltpu.get_barrier_semaphore()

    def greet(i, carry):
        pl.semaphore_signal(
            barrier, inc=1, device_id={"freq": far(i)}, device_id_type=MESH
        )
        return carry

    lax.fori_loop(0, n - 1, greet, 0, unroll=n <= 16)

    g_copy = pltpu.make_async_copy(gathers, g_buf, g_sem)
    g_copy.start()
    t_copy = pltpu.make_async_copy(waves, t_buf.at[pl.ds(0, 2 * rows)], t_sem.at[0])
    t_copy.start()
    small_copies = []
    for i, (src, dst) in enumerate(
        ((filters_hbm, filters), (lags_hbm, lags), (tile_hbm, tile_of), (len_hbm, slice_len))
    ):
        copy = pltpu.make_async_copy(src, dst, small_sem.at[i])
        copy.start()
        small_copies.append(copy)
    for m in range(slots):
        for d in range(2):
            for q in range(per_shot):
                pltpu.make_async_copy(
                    operator.at[m, d, :, pl.ds(q * traces, traces)],
                    op_bufs[2 * m + d].at[q], op_sem.at[2 * m + d],
                ).start(priority=1)
    u_copy = pltpu.make_async_copy(
        waves.at[pl.ds(0, rows)], t_buf.at[pl.ds(2 * rows, rows)], t_sem.at[1]
    )
    u_copy.start()

    g_copy.wait()
    data = g_buf[...]
    high = data.astype(jnp.bfloat16)
    low = (data - high.astype(jnp.float32)).astype(jnp.bfloat16)
    t_copy.wait()
    pairs = jnp.concatenate([high, low], axis=0)

    def transform(*totals):
        for j in range(length // MXU):
            span = slice(j * MXU, (j + 1) * MXU)
            pltpu.matmul_push_rhs(pairs[:, span], j // 2 % 2, j % 2, transpose=True)
            pltpu.matmul_acc_lhs(
                totals[j % 2], t_buf[0 : 2 * rows, span], load_staged_rhs=j // 2 % 2
            )
        p_buf[...] = pltpu.matmul_pop(totals[0]) + pltpu.matmul_pop(totals[1])

    pl.run_scoped(transform, *[pltpu.ACC(o)((2 * rows, MXU), jnp.float32) for o in range(2)])
    product = p_buf[...]
    spectrum = (
        product[0:rows, 0:traces]
        + product[0:rows, traces : 2 * traces]
        + product[rows : 2 * rows, 0:traces]
    ) * (1.0 / math.sqrt(length))
    spectrum = spectrum.astype(jnp.bfloat16)
    for d in range(n):
        send1[d] = spectrum[d * width : (d + 1) * width]

    def copy1(other):
        return pltpu.make_async_remote_copy(
            src_ref=send1.at[other], dst_ref=recv1.at[me],
            send_sem=s1, recv_sem=r1.at[me],
            device_id={"freq": other}, device_id_type=MESH,
        )

    def copy2(other):
        return pltpu.make_async_remote_copy(
            src_ref=send2.at[other], dst_ref=recv2.at[me],
            send_sem=s2, recv_sem=r2,
            device_id={"freq": other}, device_id_type=MESH,
        )

    pl.semaphore_wait(barrier, n - 1)

    def start1(i, carry):
        copy1(far(i)).start()
        return carry

    lax.fori_loop(0, n - 1, start1, 0, unroll=n <= 16)

    for copy in small_copies:
        copy.wait()

    def find(t, carry):
        at = jnp.int32(0)
        for k in range(n):
            at = jnp.where(tile_of[k] == t, k, at)
        holder[t] = at
        return carry

    lax.fori_loop(0, n, find, 0)
    spots = [holder[i] for i in range(n)]
    ends = []
    for q in range(per_shot):
        last = rank_of(spots[q])
        for s in range(1, shots):
            late = rank_of(spots[s * per_shot + q])
            last = jnp.where(late > last, late, last)
        ends.append(last)
    ranks = [
        sum([jnp.where(other < end, 1, 0) for other in ends], jnp.int32(0)) for end in ends
    ]
    for j in range(per_shot):
        at = jnp.int32(0)
        picks = [jnp.int32(0)] * shots
        for q, rank in enumerate(ranks):
            at = jnp.where(rank == j, q, at)
            picks = [
                jnp.where(rank == j, spots[s * per_shot + q], pick)
                for s, pick in enumerate(picks)
            ]
        order[j] = at
        for s, pick in enumerate(picks):
            place[s * per_shot + j] = pick

    for a in range(TAPS):
        response = lags[0] * filters[0, a, 0:1]
        for c in range(1, 4):
            response = response + lags[c] * filters[0, a, c : c + 1]
        response = jnp.sum(response, axis=1, keepdims=True)
        k_buf[a] = jnp.broadcast_to(response, (2 * rows, traces))
    if depth > 3 * rows:
        t_buf[3 * rows : depth] = jnp.zeros((depth - 3 * rows, length), jnp.bfloat16)
    x_buf[...] = jnp.zeros_like(x_buf)

    def take(i, carry):
        src = seat(i)
        pltpu.make_async_copy(send1.at[src], recv1.at[src], r1.at[src]).wait()
        x_buf[src] = recv1[src].astype(jnp.float32)
        return carry

    first = n - per_shot
    x_buf[me] = send1[me].astype(jnp.float32)
    lax.fori_loop(1, first, take, 0, unroll=n <= 16)
    row = lax.broadcasted_iota(jnp.int32, (turn, traces), 0)
    is_real = row // slots % 2 == 0
    for i, op_buf in enumerate(op_bufs):
        pltpu.make_async_copy(op_buf, op_buf, op_sem.at[i]).wait()
    tiles = receivers // MXU
    work = [(m, o) for m in range(slots) for o in range(tiles)]

    def product(*totals):
        def block(j, carry):
            q = order[j]

            def push(i):
                m, o = work[i]
                span = slice(o * MXU, (o + 1) * MXU)
                tile = jnp.concatenate([op_bufs[2 * m + d][q, span] for d in range(2)], axis=1)
                pltpu.matmul_push_rhs(tile, i // 2 % 2, o % 2, transpose=True)

            ready = 4
            for i in range(ready):
                push(i)
            take(first + j, 0)
            for s in range(shots):
                a_buf[j, s * width : (s + 1) * width] = x_buf[place[s * per_shot + j]]
            plain = a_buf[j]
            turned = jnp.where(
                is_real, -pltpu.roll(plain, turn - slots, axis=0), pltpu.roll(plain, slots, axis=0)
            )
            lefts = []
            for m in range(slots):
                pair = jnp.concatenate(
                    [jnp.where(row % slots == m, x, 0.0) for x in (plain, turned)], axis=1
                )
                if height > turn:
                    pair = jnp.concatenate(
                        [pair, jnp.zeros((height - turn, MXU), jnp.float32)], axis=0
                    )
                lefts.append(pair.astype(jnp.bfloat16))
            for i, (m, o) in enumerate(work):
                if ready == 0:
                    push(i)
                pltpu.matmul_acc_lhs(totals[o], lefts[m], load_staged_rhs=i // 2 % 2)
                if ready and i + ready < len(work):
                    push(i + ready)
            return carry

        lax.fori_loop(0, per_shot, block, 0)
        for o, total in enumerate(totals):
            a_pred[:, o * MXU : (o + 1) * MXU] = pltpu.matmul_pop(total)[0:turn]

    height = -(-turn // 16) * 16
    pl.run_scoped(
        product, *[pltpu.ACC(o % 2)((height, MXU), jnp.float32) for o in range(tiles)]
    )
    predicted = a_pred[...]
    row = lax.broadcasted_iota(jnp.int32, (turn, receivers), 0)
    predicted = jnp.where(row % slots < slice_len[me], predicted, 0.0)
    shifted = pltpu.roll(
        jnp.concatenate([predicted, jnp.zeros((turn, traces), jnp.float32)], axis=1), HALO, axis=1
    ).astype(jnp.bfloat16)
    for t in range(n):
        s, q = t // per_shot, t % per_shot
        pieces[t] = shifted[s * width : (s + 1) * width, q * traces : (q + 2) * traces]
    for k in range(n):
        send2[k] = pieces[tile_of[k]]

    def start2(i, carry):
        copy2(far(i)).start()
        return carry

    lax.fori_loop(0, n - 1, start2, 0, unroll=n <= 16)
    own2 = pltpu.make_async_copy(send2.at[me], recv2.at[me], own_sem)
    own2.start()
    u_copy.wait()
    others = pl.ds(0, n - 1)
    pltpu.make_async_copy(send1.at[others], send1.at[others], s1).wait()
    own2.wait()
    pltpu.make_async_copy(recv2.at[others], recv2.at[others], r2).wait()
    for d in range(n):
        z_buf[d * width : (d + 1) * width] = recv2[d].astype(jnp.float32)
    z = z_buf[...]
    direct = jnp.zeros((rows, traces), jnp.float32)
    cross = jnp.zeros((rows, traces), jnp.float32)
    for a in range(TAPS):
        moved = (pltpu.roll(z, 2 * traces - a, axis=1) if a else z)[:, 0:traces]
        direct = direct + k_buf[a, 0:rows] * moved
        cross = cross + k_buf[a, rows : 2 * rows] * moved
    row = lax.broadcasted_iota(jnp.int32, cross.shape, 0)
    matched = direct + jnp.where(
        row // slots % 2 == 0,
        pltpu.roll(cross, rows - slots, axis=0),
        pltpu.roll(cross, slots, axis=0),
    )
    matched = matched.T
    high = matched.astype(jnp.bfloat16)
    low = (matched - high.astype(jnp.float32)).astype(jnp.bfloat16)
    left = [high, high, low]
    if depth > 3 * rows:
        left.append(jnp.zeros((traces, depth - 3 * rows), jnp.bfloat16))
    left = jnp.concatenate(left, axis=1)
    deep = depth // MXU

    def subtract(*totals):
        def emit(j):
            span = slice(j * MXU, (j + 1) * MXU)
            out[:, span] = g_buf[:, span] - pltpu.matmul_pop(totals[j % 4])

        for j in range(length // MXU):
            if j >= 2:
                emit(j - 2)
            span = slice(j * MXU, (j + 1) * MXU)
            for i in range(deep):
                part = slice(i * MXU, (i + 1) * MXU)
                stage = (j // 2 * deep + i) % 2
                pltpu.matmul_push_rhs(t_buf[part, span], stage, j % 2)
                pltpu.matmul_acc_lhs(totals[j % 4], left[:, part], load_staged_rhs=stage)
        emit(length // MXU - 2)
        emit(length // MXU - 1)

    pl.run_scoped(subtract, *[pltpu.ACC(o % 2)((traces, MXU), jnp.float32) for o in range(4)])
    pltpu.make_async_copy(send2.at[others], send2.at[others], s2).wait()


def local(gathers, operator, filters, tile_of, slice_len):
    n = lax.axis_size("freq")
    traces, length = gathers.shape
    slots, _, receivers, _ = operator.shape
    width = 2 * slots
    rows = n * width
    per_shot = receivers // traces
    turn = n // per_shot * width
    waves = jnp.asarray(wave_table(n, slots, length))
    lags = jnp.asarray(lag_table(n, slots, length, 5 * n // 4))
    hbm = pl.BlockSpec(memory_space=pltpu.HBM)
    taps = filters.transpose(0, 2, 1, 3)
    bf16, f32 = jnp.bfloat16, jnp.float32
    dma = pltpu.SemaphoreType.DMA
    return pl.pallas_call(
        functools.partial(step, n, slots),
        out_shape=jax.ShapeDtypeStruct(gathers.shape, f32),
        in_specs=[hbm] * 7,
        out_specs=pl.BlockSpec(memory_space=pltpu.VMEM),
        scratch_shapes=[
            pltpu.VMEM((traces, length), f32),
            [pltpu.VMEM((per_shot, receivers, traces), bf16)] * (2 * slots),
            pltpu.VMEM((-(-3 * rows // MXU) * MXU, length), bf16),
            pltpu.VMEM((2 * rows, MXU), f32),
            pltpu.VMEM((n, width, traces), bf16),
            pltpu.VMEM((n, width, traces), bf16),
            pltpu.VMEM((n, width, traces), f32),
            pltpu.VMEM((per_shot, turn, traces), f32),
            pltpu.VMEM((turn, receivers), f32),
            pltpu.VMEM((n, width, 2 * traces), bf16),
            pltpu.VMEM((n, width, 2 * traces), bf16),
            pltpu.VMEM((n, width, 2 * traces), bf16),
            pltpu.VMEM((rows, 2 * traces), f32),
            pltpu.VMEM((TAPS, 2 * rows, traces), f32),
            pltpu.SMEM((n,), jnp.int32),
            pltpu.SMEM((n,), jnp.int32),
            pltpu.SMEM((per_shot,), jnp.int32),
            pltpu.VMEM(taps.shape, f32),
            pltpu.VMEM(lags.shape, f32),
            pltpu.SMEM(tile_of.shape, jnp.int32),
            pltpu.SMEM(slice_len.shape, jnp.int32),
            dma,
            dma((2 * slots,)),
            dma((2,)),
            dma((4,)),
            dma,
            dma,
            dma((n,)),
            dma,
            dma,
        ],
        compiler_params=pltpu.CompilerParams(
            collective_id=0, has_side_effects=True, vmem_limit_bytes=48*1024*1024
        ),
    )(*[pltpu.with_memory_space_constraint(x, pltpu.HBM) for x in (gathers, operator, taps, tile_of, slice_len, waves, lags)])


def solution(mesh):
    placed = (
        P(("survey", "freq"), None),
        P(("survey", "freq"), None, None, None),
        P(("survey", "freq"), None, None, None),
        P("survey"),
        P("survey"),
    )
    return jax.shard_map(
        local, mesh=mesh, in_specs=placed, out_specs=P(("survey", "freq"), None), check_vma=False
    )
```

```python
import functools
import math

import jax
import jax.numpy as jnp
import numpy as np
from jax import lax
from jax.experimental import pallas as pl
from jax.experimental.pallas import tpu as pltpu
from jax.sharding import PartitionSpec as P

FIRST = 40
TAPS = 9
HALO = 4
LAGS = 31
MXU = 256
CUTS = 2
MESH = pl.DeviceIdType.MESH


def row_bins(devices, slots):
    row = np.arange(devices * 2 * slots)
    return row // (2 * slots) * slots + row % slots, row // slots % 2


def wave_table(devices, slots, length):
    bins, part = row_bins(devices, slots)
    phase = (FIRST + bins)[:, None] * np.arange(length)[None, :] % length
    angle = 2.0 * math.pi / length * phase
    table = np.where(part[:, None] == 0, np.cos(angle), -np.sin(angle)).astype(np.float32)
    high = table.astype(jnp.bfloat16)
    low = (table - high.astype(np.float32)).astype(jnp.bfloat16)
    return np.concatenate([high, low], axis=0)


def lag_table(devices, slots, length, kept_bins):
    bins, part = row_bins(devices, slots)
    freq = FIRST + bins
    phase = freq[:, None] * (np.arange(LAGS) - LAGS // 2)[None, :] % length
    angle = 2.0 * math.pi / length * phase
    cosine, sine = np.cos(angle), np.sin(angle)
    weight = (freq / (FIRST + devices * slots))[:, None]
    real = np.stack([cosine, sine, -weight * sine, weight * cosine])
    imag = np.stack([sine, -cosine, weight * cosine, weight * sine])
    imag = np.where(part[None, :, None] == 0, imag, -imag)
    scale = math.sqrt(2.0 / kept_bins)
    return (np.concatenate([real, imag], axis=1) * scale).astype(np.float32)


def step(
    n, slots, gathers, operator, filters_hbm, tile_hbm, len_hbm, waves, lags_hbm, out,
    g_buf, op_bufs, t_buf, p_buf, send1, recv1, x_buf, a_buf, a_pred, pieces, send2, recv2,
    z_buf, k_buf, holder, place, order, filters, lags, tile_of, slice_len,
    g_sem, op_sem, t_sem, small_sem, own_sem, s1, r1, s2, r2,
):
    me = lax.axis_index("freq")
    traces, length = g_buf.shape
    receivers = op_bufs[0].shape[1]
    width = 2 * slots
    rows = n * width
    per_shot = receivers // traces
    shots = n // per_shot
    turn = shots * width
    depth = t_buf.shape[0]

    upper = me // (n // 2)
    reach = upper * (n - 1 - me) + (1 - upper) * me

    def seat(i):
        inside = (2 * reach - i + n) // n
        close = me + (1 - 2 * (i % 2)) * ((i + 1) // 2)
        return inside * close + (1 - inside) * (upper * (n - 1 - i) + (1 - upper) * i)

    def rank_of(k):
        ahead = k - me
        close = jnp.where(ahead > 0, 2 * ahead, jnp.where(ahead < 0, -2 * ahead - 1, 0))
        return jnp.where(close > 2 * reach, upper * (n - 1 - k) + (1 - upper) * k, close)

    def far(i):
        return seat(n - 1 - i)

    barrier = pltpu.get_barrier_semaphore()

    def greet(i, carry):
        pl.semaphore_signal(
            barrier, inc=1, device_id={"freq": far(i)}, device_id_type=MESH
        )
        return carry

    lax.fori_loop(0, n - 1, greet, 0, unroll=n <= 16)

    piece = length // CUTS
    g_copies, t_copies = [], []
    for j in range(CUTS):
        span = pl.ds(j * piece, piece)
        copy = pltpu.make_async_copy(gathers.at[:, span], g_buf.at[:, span], g_sem.at[j])
        copy.start()
        g_copies.append(copy)
        copy = pltpu.make_async_copy(
            waves.at[:, span], t_buf.at[pl.ds(0, 2 * rows), span], t_sem.at[j]
        )
        copy.start()
        t_copies.append(copy)
    small_copies = []
    for i, (src, dst) in enumerate(
        ((filters_hbm, filters), (lags_hbm, lags), (tile_hbm, tile_of), (len_hbm, slice_len))
    ):
        copy = pltpu.make_async_copy(src, dst, small_sem.at[i])
        copy.start()
        small_copies.append(copy)
    for m in range(slots):
        for d in range(2):
            for q in range(per_shot):
                pltpu.make_async_copy(
                    operator.at[m, d, :, pl.ds(q * traces, traces)],
                    op_bufs[2 * m + d].at[q], op_sem.at[2 * m + d],
                ).start(priority=1)
    u_copy = pltpu.make_async_copy(
        waves.at[pl.ds(0, rows)], t_buf.at[pl.ds(2 * rows, rows)], t_sem.at[CUTS]
    )
    u_copy.start()


    def transform(*totals):
        for j in range(length // MXU):
            span = slice(j * MXU, (j + 1) * MXU)
            if j * MXU % piece == 0:
                g_copies[j * MXU // piece].wait()
                t_copies[j * MXU // piece].wait()
            data = g_buf[:, span]
            high = data.astype(jnp.bfloat16)
            low = (data - high.astype(jnp.float32)).astype(jnp.bfloat16)
            pairs = jnp.concatenate([high, low], axis=0)
            pltpu.matmul_push_rhs(pairs, j // 2 % 2, j % 2, transpose=True)
            pltpu.matmul_acc_lhs(
                totals[j % 2], t_buf[0 : 2 * rows, span], load_staged_rhs=j // 2 % 2
            )
        p_buf[...] = pltpu.matmul_pop(totals[0]) + pltpu.matmul_pop(totals[1])

    pl.run_scoped(transform, *[pltpu.ACC(o)((2 * rows, MXU), jnp.float32) for o in range(2)])
    product = p_buf[...]
    spectrum = (
        product[0:rows, 0:traces]
        + product[0:rows, traces : 2 * traces]
        + product[rows : 2 * rows, 0:traces]
    ) * (1.0 / math.sqrt(length))
    spectrum = spectrum.astype(jnp.bfloat16)
    for d in range(n):
        send1[d] = spectrum[d * width : (d + 1) * width]

    def copy1(other):
        return pltpu.make_async_remote_copy(
            src_ref=send1.at[other], dst_ref=recv1.at[me],
            send_sem=s1, recv_sem=r1.at[me],
            device_id={"freq": other}, device_id_type=MESH,
        )

    def copy2(other):
        return pltpu.make_async_remote_copy(
            src_ref=send2.at[other], dst_ref=recv2.at[me],
            send_sem=s2, recv_sem=r2,
            device_id={"freq": other}, device_id_type=MESH,
        )

    pl.semaphore_wait(barrier, n - 1)

    def start1(i, carry):
        copy1(far(i)).start()
        return carry

    lax.fori_loop(0, n - 1, start1, 0, unroll=n <= 16)

    for copy in small_copies:
        copy.wait()

    def find(t, carry):
        at = jnp.int32(0)
        for k in range(n):
            at = jnp.where(tile_of[k] == t, k, at)
        holder[t] = at
        return carry

    lax.fori_loop(0, n, find, 0)
    spots = [holder[i] for i in range(n)]
    ends = []
    for q in range(per_shot):
        last = rank_of(spots[q])
        for s in range(1, shots):
            late = rank_of(spots[s * per_shot + q])
            last = jnp.where(late > last, late, last)
        ends.append(last)
    ranks = [
        sum([jnp.where(other < end, 1, 0) for other in ends], jnp.int32(0)) for end in ends
    ]
    for j in range(per_shot):
        at = jnp.int32(0)
        picks = [jnp.int32(0)] * shots
        for q, rank in enumerate(ranks):
            at = jnp.where(rank == j, q, at)
            picks = [
                jnp.where(rank == j, spots[s * per_shot + q], pick)
                for s, pick in enumerate(picks)
            ]
        order[j] = at
        for s, pick in enumerate(picks):
            place[s * per_shot + j] = pick

    for a in range(TAPS):
        response = lags[0] * filters[0, a, 0:1]
        for c in range(1, 4):
            response = response + lags[c] * filters[0, a, c : c + 1]
        response = jnp.sum(response, axis=1, keepdims=True)
        k_buf[a] = jnp.broadcast_to(response, (2 * rows, traces))
    if depth > 3 * rows:
        t_buf[3 * rows : depth] = jnp.zeros((depth - 3 * rows, length), jnp.bfloat16)
    x_buf[...] = jnp.zeros_like(x_buf)

    def take(i, carry):
        src = seat(i)
        pltpu.make_async_copy(send1.at[src], recv1.at[src], r1.at[src]).wait()
        x_buf[src] = recv1[src].astype(jnp.float32)
        return carry

    first = n - per_shot
    x_buf[me] = send1[me].astype(jnp.float32)
    lax.fori_loop(1, first, take, 0, unroll=n <= 16)
    row = lax.broadcasted_iota(jnp.int32, (turn, traces), 0)
    is_real = row // slots % 2 == 0
    for i, op_buf in enumerate(op_bufs):
        pltpu.make_async_copy(op_buf, op_buf, op_sem.at[i]).wait()
    tiles = receivers // MXU
    work = [(m, o) for m in range(slots) for o in range(tiles)]

    def product(*totals):
        def block(j, carry):
            q = order[j]

            def push(i):
                m, o = work[i]
                span = slice(o * MXU, (o + 1) * MXU)
                tile = jnp.concatenate([op_bufs[2 * m + d][q, span] for d in range(2)], axis=1)
                pltpu.matmul_push_rhs(tile, i // 2 % 2, o % 2, transpose=True)

            ready = 4
            for i in range(ready):
                push(i)
            take(first + j, 0)
            for s in range(shots):
                a_buf[j, s * width : (s + 1) * width] = x_buf[place[s * per_shot + j]]
            plain = a_buf[j]
            turned = jnp.where(
                is_real, -pltpu.roll(plain, turn - slots, axis=0), pltpu.roll(plain, slots, axis=0)
            )
            lefts = []
            for m in range(slots):
                pair = jnp.concatenate(
                    [jnp.where(row % slots == m, x, 0.0) for x in (plain, turned)], axis=1
                )
                if height > turn:
                    pair = jnp.concatenate(
                        [pair, jnp.zeros((height - turn, MXU), jnp.float32)], axis=0
                    )
                lefts.append(pair.astype(jnp.bfloat16))
            for i, (m, o) in enumerate(work):
                if ready == 0:
                    push(i)
                pltpu.matmul_acc_lhs(totals[o], lefts[m], load_staged_rhs=i // 2 % 2)
                if ready and i + ready < len(work):
                    push(i + ready)
            return carry

        lax.fori_loop(0, per_shot, block, 0)
        for o, total in enumerate(totals):
            a_pred[:, o * MXU : (o + 1) * MXU] = pltpu.matmul_pop(total)[0:turn]

    height = -(-turn // 16) * 16
    pl.run_scoped(
        product, *[pltpu.ACC(o % 2)((height, MXU), jnp.float32) for o in range(tiles)]
    )
    predicted = a_pred[...]
    row = lax.broadcasted_iota(jnp.int32, (turn, receivers), 0)
    predicted = jnp.where(row % slots < slice_len[me], predicted, 0.0)
    shifted = pltpu.roll(
        jnp.concatenate([predicted, jnp.zeros((turn, traces), jnp.float32)], axis=1), HALO, axis=1
    ).astype(jnp.bfloat16)
    for t in range(n):
        s, q = t // per_shot, t % per_shot
        pieces[t] = shifted[s * width : (s + 1) * width, q * traces : (q + 2) * traces]
    for k in range(n):
        send2[k] = pieces[tile_of[k]]

    def start2(i, carry):
        copy2(far(i)).start()
        return carry

    lax.fori_loop(0, n - 1, start2, 0, unroll=n <= 16)
    own2 = pltpu.make_async_copy(send2.at[me], recv2.at[me], own_sem)
    own2.start()
    u_copy.wait()
    others = pl.ds(0, n - 1)
    pltpu.make_async_copy(send1.at[others], send1.at[others], s1).wait()
    own2.wait()
    pltpu.make_async_copy(recv2.at[others], recv2.at[others], r2).wait()
    for d in range(n):
        z_buf[d * width : (d + 1) * width] = recv2[d].astype(jnp.float32)
    z = z_buf[...]
    direct = jnp.zeros((rows, traces), jnp.float32)
    cross = jnp.zeros((rows, traces), jnp.float32)
    for a in range(TAPS):
        moved = (pltpu.roll(z, 2 * traces - a, axis=1) if a else z)[:, 0:traces]
        direct = direct + k_buf[a, 0:rows] * moved
        cross = cross + k_buf[a, rows : 2 * rows] * moved
    row = lax.broadcasted_iota(jnp.int32, cross.shape, 0)
    matched = direct + jnp.where(
        row // slots % 2 == 0,
        pltpu.roll(cross, rows - slots, axis=0),
        pltpu.roll(cross, slots, axis=0),
    )
    matched = matched.T
    high = matched.astype(jnp.bfloat16)
    low = (matched - high.astype(jnp.float32)).astype(jnp.bfloat16)
    left = [high, high, low]
    if depth > 3 * rows:
        left.append(jnp.zeros((traces, depth - 3 * rows), jnp.bfloat16))
    left = jnp.concatenate(left, axis=1)
    deep = depth // MXU

    def subtract(*totals):
        def emit(j):
            span = slice(j * MXU, (j + 1) * MXU)
            out[:, span] = g_buf[:, span] - pltpu.matmul_pop(totals[j % 4])

        for j in range(length // MXU):
            if j >= 2:
                emit(j - 2)
            span = slice(j * MXU, (j + 1) * MXU)
            for i in range(deep):
                part = slice(i * MXU, (i + 1) * MXU)
                stage = (j // 2 * deep + i) % 2
                pltpu.matmul_push_rhs(t_buf[part, span], stage, j % 2)
                pltpu.matmul_acc_lhs(totals[j % 4], left[:, part], load_staged_rhs=stage)
        emit(length // MXU - 2)
        emit(length // MXU - 1)

    pl.run_scoped(subtract, *[pltpu.ACC(o % 2)((traces, MXU), jnp.float32) for o in range(4)])
    pltpu.make_async_copy(send2.at[others], send2.at[others], s2).wait()


def local(gathers, operator, filters, tile_of, slice_len):
    n = lax.axis_size("freq")
    traces, length = gathers.shape
    slots, _, receivers, _ = operator.shape
    width = 2 * slots
    rows = n * width
    per_shot = receivers // traces
    turn = n // per_shot * width
    waves = jnp.asarray(wave_table(n, slots, length))
    lags = jnp.asarray(lag_table(n, slots, length, 5 * n // 4))
    hbm = pl.BlockSpec(memory_space=pltpu.HBM)
    taps = filters.transpose(0, 2, 1, 3)
    bf16, f32 = jnp.bfloat16, jnp.float32
    dma = pltpu.SemaphoreType.DMA
    return pl.pallas_call(
        functools.partial(step, n, slots),
        out_shape=jax.ShapeDtypeStruct(gathers.shape, f32),
        in_specs=[hbm] * 7,
        out_specs=pl.BlockSpec(memory_space=pltpu.VMEM),
        scratch_shapes=[
            pltpu.VMEM((traces, length), f32),
            [pltpu.VMEM((per_shot, receivers, traces), bf16)] * (2 * slots),
            pltpu.VMEM((-(-3 * rows // MXU) * MXU, length), bf16),
            pltpu.VMEM((2 * rows, MXU), f32),
            pltpu.VMEM((n, width, traces), bf16),
            pltpu.VMEM((n, width, traces), bf16),
            pltpu.VMEM((n, width, traces), f32),
            pltpu.VMEM((per_shot, turn, traces), f32),
            pltpu.VMEM((turn, receivers), f32),
            pltpu.VMEM((n, width, 2 * traces), bf16),
            pltpu.VMEM((n, width, 2 * traces), bf16),
            pltpu.VMEM((n, width, 2 * traces), bf16),
            pltpu.VMEM((rows, 2 * traces), f32),
            pltpu.VMEM((TAPS, 2 * rows, traces), f32),
            pltpu.SMEM((n,), jnp.int32),
            pltpu.SMEM((n,), jnp.int32),
            pltpu.SMEM((per_shot,), jnp.int32),
            pltpu.VMEM(taps.shape, f32),
            pltpu.VMEM(lags.shape, f32),
            pltpu.SMEM(tile_of.shape, jnp.int32),
            pltpu.SMEM(slice_len.shape, jnp.int32),
            dma((CUTS,)),
            dma((2 * slots,)),
            dma((CUTS + 1,)),
            dma((4,)),
            dma,
            dma,
            dma((n,)),
            dma,
            dma,
        ],
        compiler_params=pltpu.CompilerParams(
            collective_id=0, has_side_effects=True, vmem_limit_bytes=48*1024*1024
        ),
    )(*[pltpu.with_memory_space_constraint(x, pltpu.HBM) for x in (gathers, operator, taps, tile_of, slice_len, waves, lags)])


def solution(mesh):
    placed = (
        P(("survey", "freq"), None),
        P(("survey", "freq"), None, None, None),
        P(("survey", "freq"), None, None, None),
        P("survey"),
        P("survey"),
    )
    return jax.shard_map(
        local, mesh=mesh, in_specs=placed, out_specs=P(("survey", "freq"), None), check_vma=False
    )
```

```python
import functools
import math

import jax
import jax.numpy as jnp
import numpy as np
from jax import lax
from jax.experimental import pallas as pl
from jax.experimental.pallas import tpu as pltpu
from jax.sharding import PartitionSpec as P

FIRST = 40
TAPS = 9
HALO = 4
LAGS = 31
MXU = 256
CUTS = 2
MESH = pl.DeviceIdType.MESH


def row_bins(devices, slots):
    row = np.arange(devices * 2 * slots)
    return row // (2 * slots) * slots + row % slots, row // slots % 2


def wave_table(devices, slots, length):
    bins, part = row_bins(devices, slots)
    phase = (FIRST + bins)[:, None] * np.arange(length)[None, :] % length
    angle = 2.0 * math.pi / length * phase
    table = np.where(part[:, None] == 0, np.cos(angle), -np.sin(angle)).astype(np.float32)
    high = table.astype(jnp.bfloat16)
    low = (table - high.astype(np.float32)).astype(jnp.bfloat16)
    return np.concatenate([high, low], axis=0)


def lag_table(devices, slots, length, kept_bins):
    bins, part = row_bins(devices, slots)
    freq = FIRST + bins
    phase = freq[:, None] * (np.arange(LAGS) - LAGS // 2)[None, :] % length
    angle = 2.0 * math.pi / length * phase
    cosine, sine = np.cos(angle), np.sin(angle)
    weight = (freq / (FIRST + devices * slots))[:, None]
    real = np.stack([cosine, sine, -weight * sine, weight * cosine])
    imag = np.stack([sine, -cosine, weight * cosine, weight * sine])
    imag = np.where(part[None, :, None] == 0, imag, -imag)
    scale = math.sqrt(2.0 / kept_bins)
    return (np.concatenate([real, imag], axis=1) * scale).astype(np.float32)


def step(
    n, slots, gathers, operator, filters_hbm, tile_hbm, len_hbm, waves, lags_hbm, out,
    g_buf, op_bufs, t_buf, p_buf, send1, recv1, x_buf, a_buf, a_pred, pieces, send2, recv2,
    z_buf, k_buf, holder, place, order, filters, lags, tile_of, slice_len,
    g_sem, op_sem, t_sem, small_sem, s1, r1, s2, r2,
):
    me = lax.axis_index("freq")
    traces, length = g_buf.shape
    receivers = op_bufs[0].shape[1]
    width = 2 * slots
    rows = n * width
    per_shot = receivers // traces
    shots = n // per_shot
    turn = shots * width

    upper = me // (n // 2)
    reach = upper * (n - 1 - me) + (1 - upper) * me

    def seat(i):
        inside = (2 * reach - i + n) // n
        close = me + (1 - 2 * (i % 2)) * ((i + 1) // 2)
        return inside * close + (1 - inside) * (upper * (n - 1 - i) + (1 - upper) * i)

    def rank_of(k):
        ahead = k - me
        close = jnp.where(ahead > 0, 2 * ahead, jnp.where(ahead < 0, -2 * ahead - 1, 0))
        return jnp.where(close > 2 * reach, upper * (n - 1 - k) + (1 - upper) * k, close)

    def far(i):
        return seat(n - 1 - i)

    barrier = pltpu.get_barrier_semaphore()

    def greet(i, carry):
        pl.semaphore_signal(
            barrier, inc=1, device_id={"freq": far(i)}, device_id_type=MESH
        )
        return carry

    lax.fori_loop(0, n - 1, greet, 0, unroll=n <= 16)

    piece = length // CUTS
    g_copies, t_copies = [], []
    for j in range(CUTS):
        span = pl.ds(j * piece, piece)
        copy = pltpu.make_async_copy(gathers.at[:, span], g_buf.at[:, span], g_sem.at[j])
        copy.start()
        g_copies.append(copy)
        copy = pltpu.make_async_copy(
            waves.at[:, span], t_buf.at[:, span], t_sem.at[j]
        )
        copy.start()
        t_copies.append(copy)
    small_copies = []
    for i, (src, dst) in enumerate(
        ((filters_hbm, filters), (lags_hbm, lags), (tile_hbm, tile_of), (len_hbm, slice_len))
    ):
        copy = pltpu.make_async_copy(src, dst, small_sem.at[i])
        copy.start()
        small_copies.append(copy)
    for m in range(slots):
        for d in range(2):
            for q in range(per_shot):
                pltpu.make_async_copy(
                    operator.at[m, d, :, pl.ds(q * traces, traces)],
                    op_bufs[2 * m + d].at[q], op_sem.at[2 * m + d],
                ).start(priority=1)


    def transform(*totals):
        for j in range(length // MXU):
            span = slice(j * MXU, (j + 1) * MXU)
            if j * MXU % piece == 0:
                g_copies[j * MXU // piece].wait()
                t_copies[j * MXU // piece].wait()
            data = g_buf[:, span]
            high = data.astype(jnp.bfloat16)
            low = (data - high.astype(jnp.float32)).astype(jnp.bfloat16)
            pairs = jnp.concatenate([high, low], axis=0)
            pltpu.matmul_push_rhs(pairs, j // 2 % 2, j % 2, transpose=True)
            pltpu.matmul_acc_lhs(
                totals[j % 2], t_buf[0 : 2 * rows, span], load_staged_rhs=j // 2 % 2
            )
        p_buf[...] = pltpu.matmul_pop(totals[0]) + pltpu.matmul_pop(totals[1])

    pl.run_scoped(transform, *[pltpu.ACC(o)((2 * rows, MXU), jnp.float32) for o in range(2)])
    product = p_buf[...]
    spectrum = (
        product[0:rows, 0:traces]
        + product[0:rows, traces : 2 * traces]
        + product[rows : 2 * rows, 0:traces]
    ) * (1.0 / math.sqrt(length))
    spectrum = spectrum.astype(jnp.bfloat16)
    for d in range(n):
        send1[d] = spectrum[d * width : (d + 1) * width]

    def copy1(other):
        return pltpu.make_async_remote_copy(
            src_ref=send1.at[other], dst_ref=recv1.at[me],
            send_sem=s1, recv_sem=r1.at[me],
            device_id={"freq": other}, device_id_type=MESH,
        )

    def copy2(other):
        return pltpu.make_async_remote_copy(
            src_ref=send2.at[other], dst_ref=recv2.at[me],
            send_sem=s2, recv_sem=r2.at[upper],
            device_id={"freq": other}, device_id_type=MESH,
        )

    pl.semaphore_wait(barrier, n - 1)

    def start1(i, carry):
        copy1(far(i)).start()
        return carry

    lax.fori_loop(0, n - 1, start1, 0, unroll=n <= 16)

    for copy in small_copies:
        copy.wait()

    def find(t, carry):
        at = jnp.int32(0)
        for k in range(n):
            at = jnp.where(tile_of[k] == t, k, at)
        holder[t] = at
        return carry

    lax.fori_loop(0, n, find, 0)
    spots = [holder[i] for i in range(n)]
    ends = []
    for q in range(per_shot):
        last = rank_of(spots[q])
        for s in range(1, shots):
            late = rank_of(spots[s * per_shot + q])
            last = jnp.where(late > last, late, last)
        ends.append(last)
    ranks = [
        sum([jnp.where(other < end, 1, 0) for other in ends], jnp.int32(0)) for end in ends
    ]
    for j in range(per_shot):
        at = jnp.int32(0)
        picks = [jnp.int32(0)] * shots
        for q, rank in enumerate(ranks):
            at = jnp.where(rank == j, q, at)
            picks = [
                jnp.where(rank == j, spots[s * per_shot + q], pick)
                for s, pick in enumerate(picks)
            ]
        order[j] = at
        for s, pick in enumerate(picks):
            place[s * per_shot + j] = pick

    for a in range(TAPS):
        response = lags[0] * filters[0, a, 0:1]
        for c in range(1, 4):
            response = response + lags[c] * filters[0, a, c : c + 1]
        response = jnp.sum(response, axis=1, keepdims=True)
        k_buf[a] = jnp.broadcast_to(response, (2 * rows, traces))
    x_buf[...] = jnp.zeros_like(x_buf)

    def take(i, carry):
        src = seat(i)
        pltpu.make_async_copy(send1.at[src], recv1.at[src], r1.at[src]).wait()
        x_buf[src] = recv1[src].astype(jnp.float32)
        return carry

    first = n - per_shot
    x_buf[me] = send1[me].astype(jnp.float32)
    lax.fori_loop(1, first, take, 0, unroll=n <= 16)
    row = lax.broadcasted_iota(jnp.int32, (turn, traces), 0)
    is_real = row // slots % 2 == 0
    for i, op_buf in enumerate(op_bufs):
        pltpu.make_async_copy(op_buf, op_buf, op_sem.at[i]).wait()
    tiles = receivers // MXU
    work = [(m, o) for m in range(slots) for o in range(tiles)]

    def product(*totals):
        def block(j, carry):
            q = order[j]

            def push(i):
                m, o = work[i]
                span = slice(o * MXU, (o + 1) * MXU)
                tile = jnp.concatenate([op_bufs[2 * m + d][q, span] for d in range(2)], axis=1)
                pltpu.matmul_push_rhs(tile, i // 2 % 2, o % 2, transpose=True)

            ready = 4
            for i in range(ready):
                push(i)
            take(first + j, 0)
            for s in range(shots):
                a_buf[j, s * width : (s + 1) * width] = x_buf[place[s * per_shot + j]]
            plain = a_buf[j]
            turned = jnp.where(
                is_real, -pltpu.roll(plain, turn - slots, axis=0), pltpu.roll(plain, slots, axis=0)
            )
            lefts = []
            for m in range(slots):
                pair = jnp.concatenate(
                    [jnp.where(row % slots == m, x, 0.0) for x in (plain, turned)], axis=1
                )
                if height > turn:
                    pair = jnp.concatenate(
                        [pair, jnp.zeros((height - turn, MXU), jnp.float32)], axis=0
                    )
                lefts.append(pair.astype(jnp.bfloat16))
            for i, (m, o) in enumerate(work):
                if ready == 0:
                    push(i)
                pltpu.matmul_acc_lhs(totals[o], lefts[m], load_staged_rhs=i // 2 % 2)
                if ready and i + ready < len(work):
                    push(i + ready)
            return carry

        lax.fori_loop(0, per_shot, block, 0)
        for o, total in enumerate(totals):
            a_pred[:, o * MXU : (o + 1) * MXU] = pltpu.matmul_pop(total)[0:turn]

    height = -(-turn // 16) * 16
    pl.run_scoped(
        product, *[pltpu.ACC(o % 2)((height, MXU), jnp.float32) for o in range(tiles)]
    )
    predicted = a_pred[...]
    row = lax.broadcasted_iota(jnp.int32, (turn, receivers), 0)
    predicted = jnp.where(row % slots < slice_len[me], predicted, 0.0)
    shifted = pltpu.roll(
        jnp.concatenate([predicted, jnp.zeros((turn, traces), jnp.float32)], axis=1), HALO, axis=1
    ).astype(jnp.bfloat16)
    for t in range(n):
        s, q = t // per_shot, t % per_shot
        pieces[t] = shifted[s * width : (s + 1) * width, q * traces : (q + 2) * traces]

    def start2(i, carry):
        other = far(i)
        send2[other] = pieces[tile_of[other]]
        copy2(other).start()
        return carry

    lax.fori_loop(0, n - 1, start2, 0, unroll=n <= 16)
    recv2[me] = pieces[tile_of[me]]
    others = pl.ds(0, n - 1)
    pltpu.make_async_copy(send1.at[others], send1.at[others], s1).wait()
    half = n // 2
    lanes = half * width
    depth = -(-3 * lanes // MXU) * MXU

    def match(side):
        base = pl.multiple_of(side * lanes, lanes)
        for d in range(half):
            z_buf[d * width : (d + 1) * width] = recv2[side * half + d].astype(jnp.float32)
        z = z_buf[...]
        direct = jnp.zeros((lanes, traces), jnp.float32)
        cross = jnp.zeros((lanes, traces), jnp.float32)
        for a in range(TAPS):
            moved = (pltpu.roll(z, 2 * traces - a, axis=1) if a else z)[:, 0:traces]
            direct = direct + k_buf[a, pl.ds(base, lanes)] * moved
            cross = cross + k_buf[a, pl.ds(rows + base, lanes)] * moved
        row = lax.broadcasted_iota(jnp.int32, cross.shape, 0)
        matched = direct + jnp.where(
            row // slots % 2 == 0,
            pltpu.roll(cross, lanes - slots, axis=0),
            pltpu.roll(cross, slots, axis=0),
        )
        matched = matched.T
        high = matched.astype(jnp.bfloat16)
        low = (matched - high.astype(jnp.float32)).astype(jnp.bfloat16)
        left = [high, high, low]
        if depth > 3 * lanes:
            left.append(jnp.zeros((traces, depth - 3 * lanes), jnp.bfloat16))
        return base, jnp.concatenate(left, axis=1)

    def subtract(*totals):
        def add(j, base, left, turn_of):
            span = slice(j * MXU, (j + 1) * MXU)
            high = t_buf[pl.ds(base, lanes), span]
            low = t_buf[pl.ds(rows + base, lanes), span]
            right = [high, low, high]
            if depth > 3 * lanes:
                right.append(jnp.zeros((depth - 3 * lanes, MXU), jnp.bfloat16))
            right = jnp.concatenate(right, axis=0)
            for i in range(depth // MXU):
                part = slice(i * MXU, (i + 1) * MXU)
                stage = (turn_of * (depth // MXU) + i) % 2
                pltpu.matmul_push_rhs(right[part], stage, j % 2)
                pltpu.matmul_acc_lhs(totals[j], left[:, part], load_staged_rhs=stage)

        def emit(j):
            span = slice(j * MXU, (j + 1) * MXU)
            out[:, span] = g_buf[:, span] - pltpu.matmul_pop(totals[j])

        count = length // MXU
        near = pl.ds(0, half - 1)
        pltpu.make_async_copy(recv2.at[near], recv2.at[near], r2.at[upper]).wait()
        base, left = match(upper)
        for j in range(count):
            add(j, base, left, j // 2)
        rest = pl.ds(0, half)
        pltpu.make_async_copy(recv2.at[rest], recv2.at[rest], r2.at[1 - upper]).wait()
        base, left = match(1 - upper)
        for j in range(count):
            add(j, base, left, (count + j) // 2)
            if j >= 2:
                emit(j - 2)
        emit(count - 2)
        emit(count - 1)

    pl.run_scoped(
        subtract,
        *[pltpu.ACC(j % 2)((traces, MXU), jnp.float32) for j in range(length // MXU)],
    )
    pltpu.make_async_copy(send2.at[others], send2.at[others], s2).wait()


def local(gathers, operator, filters, tile_of, slice_len):
    n = lax.axis_size("freq")
    traces, length = gathers.shape
    slots, _, receivers, _ = operator.shape
    width = 2 * slots
    rows = n * width
    per_shot = receivers // traces
    turn = n // per_shot * width
    waves = jnp.asarray(wave_table(n, slots, length))
    lags = jnp.asarray(lag_table(n, slots, length, 5 * n // 4))
    hbm = pl.BlockSpec(memory_space=pltpu.HBM)
    taps = filters.transpose(0, 2, 1, 3)
    bf16, f32 = jnp.bfloat16, jnp.float32
    dma = pltpu.SemaphoreType.DMA
    return pl.pallas_call(
        functools.partial(step, n, slots),
        out_shape=jax.ShapeDtypeStruct(gathers.shape, f32),
        in_specs=[hbm] * 7,
        out_specs=pl.BlockSpec(memory_space=pltpu.VMEM),
        scratch_shapes=[
            pltpu.VMEM((traces, length), f32),
            [pltpu.VMEM((per_shot, receivers, traces), bf16)] * (2 * slots),
            pltpu.VMEM((2 * rows, length), bf16),
            pltpu.VMEM((2 * rows, MXU), f32),
            pltpu.VMEM((n, width, traces), bf16),
            pltpu.VMEM((n, width, traces), bf16),
            pltpu.VMEM((n, width, traces), f32),
            pltpu.VMEM((per_shot, turn, traces), f32),
            pltpu.VMEM((turn, receivers), f32),
            pltpu.VMEM((n, width, 2 * traces), bf16),
            pltpu.VMEM((n, width, 2 * traces), bf16),
            pltpu.VMEM((n, width, 2 * traces), bf16),
            pltpu.VMEM((rows // 2, 2 * traces), f32),
            pltpu.VMEM((TAPS, 2 * rows, traces), f32),
            pltpu.SMEM((n,), jnp.int32),
            pltpu.SMEM((n,), jnp.int32),
            pltpu.SMEM((per_shot,), jnp.int32),
            pltpu.VMEM(taps.shape, f32),
            pltpu.VMEM(lags.shape, f32),
            pltpu.SMEM(tile_of.shape, jnp.int32),
            pltpu.SMEM(slice_len.shape, jnp.int32),
            dma((CUTS,)),
            dma((2 * slots,)),
            dma((CUTS,)),
            dma((4,)),
            dma,
            dma((n,)),
            dma,
            dma((2,)),
        ],
        compiler_params=pltpu.CompilerParams(
            collective_id=0, has_side_effects=True, vmem_limit_bytes=48*1024*1024
        ),
    )(*[pltpu.with_memory_space_constraint(x, pltpu.HBM) for x in (gathers, operator, taps, tile_of, slice_len, waves, lags)])


def solution(mesh):
    placed = (
        P(("survey", "freq"), None),
        P(("survey", "freq"), None, None, None),
        P(("survey", "freq"), None, None, None),
        P("survey"),
        P("survey"),
    )
    return jax.shard_map(
        local, mesh=mesh, in_specs=placed, out_specs=P(("survey", "freq"), None), check_vma=False
    )
```

```python
import functools
import math

import jax
import jax.numpy as jnp
import numpy as np
from jax import lax
from jax.experimental import pallas as pl
from jax.experimental.pallas import tpu as pltpu
from jax.sharding import PartitionSpec as P

FIRST = 40
TAPS = 9
HALO = 4
LAGS = 31
MXU = 256
CUTS = 2
MESH = pl.DeviceIdType.MESH


def row_bins(devices, slots):
    row = np.arange(devices * 2 * slots)
    return row // (2 * slots) * slots + row % slots, row // slots % 2


def wave_table(devices, slots, length):
    bins, part = row_bins(devices, slots)
    phase = (FIRST + bins)[:, None] * np.arange(length)[None, :] % length
    angle = 2.0 * math.pi / length * phase
    table = np.where(part[:, None] == 0, np.cos(angle), -np.sin(angle)).astype(np.float32)
    high = table.astype(jnp.bfloat16)
    low = (table - high.astype(np.float32)).astype(jnp.bfloat16)
    return np.concatenate([high, low], axis=0)


def lag_table(devices, slots, length, kept_bins):
    bins, part = row_bins(devices, slots)
    freq = FIRST + bins
    phase = freq[:, None] * (np.arange(LAGS) - LAGS // 2)[None, :] % length
    angle = 2.0 * math.pi / length * phase
    cosine, sine = np.cos(angle), np.sin(angle)
    weight = (freq / (FIRST + devices * slots))[:, None]
    real = np.stack([cosine, sine, -weight * sine, weight * cosine])
    imag = np.stack([sine, -cosine, weight * cosine, weight * sine])
    imag = np.where(part[None, :, None] == 0, imag, -imag)
    scale = math.sqrt(2.0 / kept_bins)
    return (np.concatenate([real, imag], axis=1) * scale).astype(np.float32)


def step(
    n, slots, gathers, operator, filters_hbm, tile_hbm, len_hbm, waves, lags_hbm, out,
    g_buf, op_bufs, swapped, t_buf, p_buf, send1, recv1, x_buf, a_buf, a_pred, pieces, send2, recv2,
    z_buf, k_buf, holder, place, order, filters, lags, tile_of, slice_len,
    g_sem, op_sem, t_sem, small_sem, s1, r1, s2, r2,
):
    me = lax.axis_index("freq")
    traces, length = g_buf.shape
    receivers = op_bufs[0].shape[1]
    width = 2 * slots
    rows = n * width
    per_shot = receivers // traces
    shots = n // per_shot
    turn = shots * width

    upper = me // (n // 2)
    reach = upper * (n - 1 - me) + (1 - upper) * me

    def seat(i):
        inside = (2 * reach - i + n) // n
        close = me + (1 - 2 * (i % 2)) * ((i + 1) // 2)
        return inside * close + (1 - inside) * (upper * (n - 1 - i) + (1 - upper) * i)

    def rank_of(k):
        ahead = k - me
        close = jnp.where(ahead > 0, 2 * ahead, jnp.where(ahead < 0, -2 * ahead - 1, 0))
        return jnp.where(close > 2 * reach, upper * (n - 1 - k) + (1 - upper) * k, close)

    def far(i):
        return seat(n - 1 - i)

    barrier = pltpu.get_barrier_semaphore()

    def greet(i, carry):
        pl.semaphore_signal(
            barrier, inc=1, device_id={"freq": far(i)}, device_id_type=MESH
        )
        return carry

    lax.fori_loop(0, n - 1, greet, 0, unroll=n <= 16)

    piece = length // CUTS
    g_copies, t_copies = [], []
    for j in range(CUTS):
        span = pl.ds(j * piece, piece)
        copy = pltpu.make_async_copy(gathers.at[:, span], g_buf.at[:, span], g_sem.at[j])
        copy.start()
        g_copies.append(copy)
        copy = pltpu.make_async_copy(
            waves.at[:, span], t_buf.at[:, span], t_sem.at[j]
        )
        copy.start()
        t_copies.append(copy)
    small_copies = []
    for i, (src, dst) in enumerate(
        ((filters_hbm, filters), (lags_hbm, lags), (tile_hbm, tile_of), (len_hbm, slice_len))
    ):
        copy = pltpu.make_async_copy(src, dst, small_sem.at[i])
        copy.start()
        small_copies.append(copy)
    for m in range(slots):
        for d in range(2):
            for q in range(per_shot):
                pltpu.make_async_copy(
                    operator.at[m, d, :, pl.ds(q * traces, traces)],
                    op_bufs[2 * m + d].at[q], op_sem.at[2 * m + d],
                ).start(priority=1)


    def transform(*totals):
        for j in range(length // MXU):
            span = slice(j * MXU, (j + 1) * MXU)
            if j * MXU % piece == 0:
                g_copies[j * MXU // piece].wait()
                t_copies[j * MXU // piece].wait()
            data = g_buf[:, span]
            high = data.astype(jnp.bfloat16)
            low = (data - high.astype(jnp.float32)).astype(jnp.bfloat16)
            pairs = jnp.concatenate([high, low], axis=0)
            pltpu.matmul_push_rhs(pairs, j // 2 % 2, j % 2, transpose=True)
            pltpu.matmul_acc_lhs(
                totals[j % 2], t_buf[0 : 2 * rows, span], load_staged_rhs=j // 2 % 2
            )
        p_buf[...] = pltpu.matmul_pop(totals[0]) + pltpu.matmul_pop(totals[1])

    pl.run_scoped(transform, *[pltpu.ACC(o)((2 * rows, MXU), jnp.float32) for o in range(2)])
    product = p_buf[...]
    spectrum = (
        product[0:rows, 0:traces]
        + product[0:rows, traces : 2 * traces]
        + product[rows : 2 * rows, 0:traces]
    ) * (1.0 / math.sqrt(length))
    spectrum = spectrum.astype(jnp.bfloat16)
    for d in range(n):
        send1[d] = spectrum[d * width : (d + 1) * width]

    def copy1(other):
        return pltpu.make_async_remote_copy(
            src_ref=send1.at[other], dst_ref=recv1.at[me],
            send_sem=s1, recv_sem=r1.at[me],
            device_id={"freq": other}, device_id_type=MESH,
        )

    def copy2(other):
        return pltpu.make_async_remote_copy(
            src_ref=send2.at[other], dst_ref=recv2.at[me],
            send_sem=s2, recv_sem=r2.at[upper],
            device_id={"freq": other}, device_id_type=MESH,
        )

    pl.semaphore_wait(barrier, n - 1)

    def start1(i, carry):
        copy1(far(i)).start()
        return carry

    lax.fori_loop(0, n - 1, start1, 0, unroll=n <= 16)

    for copy in small_copies:
        copy.wait()

    def find(t, carry):
        at = jnp.int32(0)
        for k in range(n):
            at = jnp.where(tile_of[k] == t, k, at)
        holder[t] = at
        return carry

    lax.fori_loop(0, n, find, 0)
    spots = [holder[i] for i in range(n)]
    ends = []
    for q in range(per_shot):
        last = rank_of(spots[q])
        for s in range(1, shots):
            late = rank_of(spots[s * per_shot + q])
            last = jnp.where(late > last, late, last)
        ends.append(last)
    ranks = [
        sum([jnp.where(other < end, 1, 0) for other in ends], jnp.int32(0)) for end in ends
    ]
    for j in range(per_shot):
        at = jnp.int32(0)
        picks = [jnp.int32(0)] * shots
        for q, rank in enumerate(ranks):
            at = jnp.where(rank == j, q, at)
            picks = [
                jnp.where(rank == j, spots[s * per_shot + q], pick)
                for s, pick in enumerate(picks)
            ]
        order[j] = at
        for s, pick in enumerate(picks):
            place[s * per_shot + j] = pick

    x_buf[...] = jnp.zeros_like(x_buf)

    for d in range(2):
        pltpu.make_async_copy(op_bufs[d], op_bufs[d], op_sem.at[d]).wait()

    def swap(q, carry):
        for d in range(2):
            swapped[d, q] = op_bufs[d][q].T
        return carry

    lax.fori_loop(0, per_shot, swap, 0, unroll=2)

    def take(i, carry):
        src = seat(i)
        pltpu.make_async_copy(send1.at[src], recv1.at[src], r1.at[src]).wait()
        x_buf[src] = recv1[src].astype(jnp.float32)
        return carry

    first = n - per_shot
    x_buf[me] = send1[me].astype(jnp.float32)
    lax.fori_loop(1, first, take, 0, unroll=n <= 16)
    row = lax.broadcasted_iota(jnp.int32, (turn, traces), 0)
    is_real = row // slots % 2 == 0
    for i in range(2, 2 * slots):
        pltpu.make_async_copy(op_bufs[i], op_bufs[i], op_sem.at[i]).wait()
    tiles = receivers // MXU
    work = [(m, o) for m in reversed(range(slots)) for o in range(tiles)]

    def product(*totals):
        def block(j, carry):
            q = order[j]

            def push(i):
                m, o = work[i]
                span = slice(o * MXU, (o + 1) * MXU)
                if m == 0:
                    tile = jnp.concatenate([swapped[d, q, :, span] for d in range(2)], axis=0)
                else:
                    tile = jnp.concatenate([op_bufs[2 * m + d][q, span] for d in range(2)], axis=1)
                pltpu.matmul_push_rhs(tile, i // 2 % 2, o % 2, transpose=m > 0)

            ready = 4
            for i in range(ready):
                push(i)
            take(first + j, 0)
            for s in range(shots):
                a_buf[j, s * width : (s + 1) * width] = x_buf[place[s * per_shot + j]]
            plain = a_buf[j]
            turned = jnp.where(
                is_real, -pltpu.roll(plain, turn - slots, axis=0), pltpu.roll(plain, slots, axis=0)
            )
            lefts = []
            for m in range(slots):
                pair = jnp.concatenate(
                    [jnp.where(row % slots == m, x, 0.0) for x in (plain, turned)], axis=1
                )
                if height > turn:
                    pair = jnp.concatenate(
                        [pair, jnp.zeros((height - turn, MXU), jnp.float32)], axis=0
                    )
                lefts.append(pair.astype(jnp.bfloat16))
            for i, (m, o) in enumerate(work):
                if ready == 0:
                    push(i)
                pltpu.matmul_acc_lhs(totals[o], lefts[m], load_staged_rhs=i // 2 % 2)
                if ready and i + ready < len(work):
                    push(i + ready)
            return carry

        lax.fori_loop(0, per_shot, block, 0)
        for o, total in enumerate(totals):
            a_pred[:, o * MXU : (o + 1) * MXU] = pltpu.matmul_pop(total)[0:turn]

    height = -(-turn // 16) * 16
    pl.run_scoped(
        product, *[pltpu.ACC(o % 2)((height, MXU), jnp.float32) for o in range(tiles)]
    )
    predicted = a_pred[...]
    row = lax.broadcasted_iota(jnp.int32, (turn, receivers), 0)
    predicted = jnp.where(row % slots < slice_len[me], predicted, 0.0)
    shifted = pltpu.roll(
        jnp.concatenate([predicted, jnp.zeros((turn, traces), jnp.float32)], axis=1), HALO, axis=1
    ).astype(jnp.bfloat16)
    for t in range(n):
        s, q = t // per_shot, t % per_shot
        pieces[t] = shifted[s * width : (s + 1) * width, q * traces : (q + 2) * traces]

    def start2(i, carry):
        other = far(i)
        send2[other] = pieces[tile_of[other]]
        copy2(other).start()
        return carry

    lax.fori_loop(0, n - 1, start2, 0, unroll=n <= 16)
    recv2[me] = pieces[tile_of[me]]
    for a in range(TAPS):
        response = lags[0] * filters[0, a, 0:1]
        for c in range(1, 4):
            response = response + lags[c] * filters[0, a, c : c + 1]
        response = jnp.sum(response, axis=1, keepdims=True)
        k_buf[a] = jnp.broadcast_to(response, (2 * rows, traces))
    others = pl.ds(0, n - 1)
    pltpu.make_async_copy(send1.at[others], send1.at[others], s1).wait()
    half = n // 2
    lanes = half * width
    depth = -(-3 * lanes // MXU) * MXU

    def match(side):
        base = pl.multiple_of(side * lanes, lanes)
        for d in range(half):
            z_buf[d * width : (d + 1) * width] = recv2[side * half + d].astype(jnp.float32)
        z = z_buf[...]
        direct = jnp.zeros((lanes, traces), jnp.float32)
        cross = jnp.zeros((lanes, traces), jnp.float32)
        for a in range(TAPS):
            moved = (pltpu.roll(z, 2 * traces - a, axis=1) if a else z)[:, 0:traces]
            direct = direct + k_buf[a, pl.ds(base, lanes)] * moved
            cross = cross + k_buf[a, pl.ds(rows + base, lanes)] * moved
        row = lax.broadcasted_iota(jnp.int32, cross.shape, 0)
        matched = direct + jnp.where(
            row // slots % 2 == 0,
            pltpu.roll(cross, lanes - slots, axis=0),
            pltpu.roll(cross, slots, axis=0),
        )
        matched = matched.T
        high = matched.astype(jnp.bfloat16)
        low = (matched - high.astype(jnp.float32)).astype(jnp.bfloat16)
        left = [high, high, low]
        if depth > 3 * lanes:
            left.append(jnp.zeros((traces, depth - 3 * lanes), jnp.bfloat16))
        return base, jnp.concatenate(left, axis=1)

    def subtract(*totals):
        def add(j, base, left, turn_of):
            span = slice(j * MXU, (j + 1) * MXU)
            high = t_buf[pl.ds(base, lanes), span]
            low = t_buf[pl.ds(rows + base, lanes), span]
            right = [high, low, high]
            if depth > 3 * lanes:
                right.append(jnp.zeros((depth - 3 * lanes, MXU), jnp.bfloat16))
            right = jnp.concatenate(right, axis=0)
            for i in range(depth // MXU):
                part = slice(i * MXU, (i + 1) * MXU)
                stage = (turn_of * (depth // MXU) + i) % 2
                pltpu.matmul_push_rhs(right[part], stage, j % 2)
                pltpu.matmul_acc_lhs(totals[j], left[:, part], load_staged_rhs=stage)

        def emit(j):
            span = slice(j * MXU, (j + 1) * MXU)
            out[:, span] = g_buf[:, span] - pltpu.matmul_pop(totals[j])

        count = length // MXU
        near = pl.ds(0, half - 1)
        pltpu.make_async_copy(recv2.at[near], recv2.at[near], r2.at[upper]).wait()
        base, left = match(upper)
        for j in range(count):
            add(j, base, left, j // 2)
        rest = pl.ds(0, half)
        pltpu.make_async_copy(recv2.at[rest], recv2.at[rest], r2.at[1 - upper]).wait()
        base, left = match(1 - upper)
        for j in range(count):
            add(j, base, left, (count + j) // 2)
            if j >= 2:
                emit(j - 2)
        emit(count - 2)
        emit(count - 1)

    pl.run_scoped(
        subtract,
        *[pltpu.ACC(j % 2)((traces, MXU), jnp.float32) for j in range(length // MXU)],
    )
    pltpu.make_async_copy(send2.at[others], send2.at[others], s2).wait()


def local(gathers, operator, filters, tile_of, slice_len):
    n = lax.axis_size("freq")
    traces, length = gathers.shape
    slots, _, receivers, _ = operator.shape
    width = 2 * slots
    rows = n * width
    per_shot = receivers // traces
    turn = n // per_shot * width
    waves = jnp.asarray(wave_table(n, slots, length))
    lags = jnp.asarray(lag_table(n, slots, length, 5 * n // 4))
    hbm = pl.BlockSpec(memory_space=pltpu.HBM)
    taps = filters.transpose(0, 2, 1, 3)
    bf16, f32 = jnp.bfloat16, jnp.float32
    dma = pltpu.SemaphoreType.DMA
    return pl.pallas_call(
        functools.partial(step, n, slots),
        out_shape=jax.ShapeDtypeStruct(gathers.shape, f32),
        in_specs=[hbm] * 7,
        out_specs=pl.BlockSpec(memory_space=pltpu.VMEM),
        scratch_shapes=[
            pltpu.VMEM((traces, length), f32),
            [pltpu.VMEM((per_shot, receivers, traces), bf16)] * (2 * slots),
            pltpu.VMEM((2, per_shot, traces, receivers), bf16),
            pltpu.VMEM((2 * rows, length), bf16),
            pltpu.VMEM((2 * rows, MXU), f32),
            pltpu.VMEM((n, width, traces), bf16),
            pltpu.VMEM((n, width, traces), bf16),
            pltpu.VMEM((n, width, traces), f32),
            pltpu.VMEM((per_shot, turn, traces), f32),
            pltpu.VMEM((turn, receivers), f32),
            pltpu.VMEM((n, width, 2 * traces), bf16),
            pltpu.VMEM((n, width, 2 * traces), bf16),
            pltpu.VMEM((n, width, 2 * traces), bf16),
            pltpu.VMEM((rows // 2, 2 * traces), f32),
            pltpu.VMEM((TAPS, 2 * rows, traces), f32),
            pltpu.SMEM((n,), jnp.int32),
            pltpu.SMEM((n,), jnp.int32),
            pltpu.SMEM((per_shot,), jnp.int32),
            pltpu.VMEM(taps.shape, f32),
            pltpu.VMEM(lags.shape, f32),
            pltpu.SMEM(tile_of.shape, jnp.int32),
            pltpu.SMEM(slice_len.shape, jnp.int32),
            dma((CUTS,)),
            dma((2 * slots,)),
            dma((CUTS,)),
            dma((4,)),
            dma,
            dma((n,)),
            dma,
            dma((2,)),
        ],
        compiler_params=pltpu.CompilerParams(
            collective_id=0, has_side_effects=True, vmem_limit_bytes=48*1024*1024
        ),
    )(*[pltpu.with_memory_space_constraint(x, pltpu.HBM) for x in (gathers, operator, taps, tile_of, slice_len, waves, lags)])


def solution(mesh):
    placed = (
        P(("survey", "freq"), None),
        P(("survey", "freq"), None, None, None),
        P(("survey", "freq"), None, None, None),
        P("survey"),
        P("survey"),
    )
    return jax.shard_map(
        local, mesh=mesh, in_specs=placed, out_specs=P(("survey", "freq"), None), check_vma=False
    )
```

```python
import functools
import math

import jax
import jax.numpy as jnp
import numpy as np
from jax import lax
from jax.experimental import pallas as pl
from jax.experimental.pallas import tpu as pltpu
from jax.sharding import PartitionSpec as P

FIRST = 40
TAPS = 9
HALO = 4
LAGS = 31
MXU = 256
CUTS = 2
MESH = pl.DeviceIdType.MESH


def row_bins(devices, slots):
    row = np.arange(devices * 2 * slots)
    return row // (2 * slots) * slots + row % slots, row // slots % 2


def wave_table(devices, slots, length):
    bins, part = row_bins(devices, slots)
    phase = (FIRST + bins)[:, None] * np.arange(length)[None, :] % length
    angle = 2.0 * math.pi / length * phase
    table = np.where(part[:, None] == 0, np.cos(angle), -np.sin(angle)).astype(np.float32)
    high = table.astype(jnp.bfloat16)
    low = (table - high.astype(np.float32)).astype(jnp.bfloat16)
    return np.concatenate([high, low], axis=0)


def lag_table(devices, slots, length, kept_bins):
    bins, part = row_bins(devices, slots)
    freq = FIRST + bins
    phase = freq[:, None] * (np.arange(LAGS) - LAGS // 2)[None, :] % length
    angle = 2.0 * math.pi / length * phase
    cosine, sine = np.cos(angle), np.sin(angle)
    weight = (freq / (FIRST + devices * slots))[:, None]
    real = np.stack([cosine, sine, -weight * sine, weight * cosine])
    imag = np.stack([sine, -cosine, weight * cosine, weight * sine])
    imag = np.where(part[None, :, None] == 0, imag, -imag)
    scale = math.sqrt(2.0 / kept_bins)
    return (np.concatenate([real, imag], axis=1) * scale).astype(np.float32)


def step(
    n, slots, gathers, operator, filters_hbm, tile_hbm, len_hbm, waves, lags_hbm, out,
    g_buf, op_bufs, swapped, t_buf, p_buf, send1, recv1, x_buf, a_buf, a_pred, pieces, send2, recv2,
    z_buf, k_buf, holder, place, order, filters, lags, tile_of, slice_len,
    g_sem, op_sem, t_sem, small_sem, s1, r1, s2, r2,
):
    me = lax.axis_index("freq")
    traces, length = g_buf.shape
    receivers = op_bufs[0].shape[1]
    width = 2 * slots
    rows = n * width
    per_shot = receivers // traces
    shots = n // per_shot
    turn = shots * width

    upper = me // (n // 2)
    reach = upper * (n - 1 - me) + (1 - upper) * me

    def seat(i):
        inside = (2 * reach - i + n) // n
        close = me + (1 - 2 * (i % 2)) * ((i + 1) // 2)
        return inside * close + (1 - inside) * (upper * (n - 1 - i) + (1 - upper) * i)

    def rank_of(k):
        ahead = k - me
        close = jnp.where(ahead > 0, 2 * ahead, jnp.where(ahead < 0, -2 * ahead - 1, 0))
        return jnp.where(close > 2 * reach, upper * (n - 1 - k) + (1 - upper) * k, close)

    def far(i):
        return seat(n - 1 - i)

    barrier = pltpu.get_barrier_semaphore()

    def greet(i, carry):
        pl.semaphore_signal(
            barrier, inc=1, device_id={"freq": far(i)}, device_id_type=MESH
        )
        return carry

    lax.fori_loop(0, n - 1, greet, 0, unroll=n <= 16)

    piece = length // CUTS
    g_copies, t_copies = [], []
    for j in range(CUTS):
        span = pl.ds(j * piece, piece)
        copy = pltpu.make_async_copy(gathers.at[:, span], g_buf.at[:, span], g_sem.at[j])
        copy.start()
        g_copies.append(copy)
        copy = pltpu.make_async_copy(
            waves.at[:, span], t_buf.at[:, span], t_sem.at[j]
        )
        copy.start()
        t_copies.append(copy)
    small_copies = []
    for i, (src, dst) in enumerate(
        ((filters_hbm, filters), (lags_hbm, lags), (tile_hbm, tile_of), (len_hbm, slice_len))
    ):
        copy = pltpu.make_async_copy(src, dst, small_sem.at[i])
        copy.start()
        small_copies.append(copy)
    for m in range(slots):
        for d in range(2):
            for q in range(per_shot):
                pltpu.make_async_copy(
                    operator.at[m, d, :, pl.ds(q * traces, traces)],
                    op_bufs[2 * m + d].at[q], op_sem.at[2 * m + d],
                ).start(priority=1)


    def transform(*totals):
        for j in range(length // MXU):
            span = slice(j * MXU, (j + 1) * MXU)
            if j * MXU % piece == 0:
                g_copies[j * MXU // piece].wait()
                t_copies[j * MXU // piece].wait()
            data = g_buf[:, span]
            high = data.astype(jnp.bfloat16)
            low = (data - high.astype(jnp.float32)).astype(jnp.bfloat16)
            pairs = jnp.concatenate([high, low], axis=0)
            pltpu.matmul_push_rhs(pairs, j // 2 % 2, j % 2, transpose=True)
            pltpu.matmul_acc_lhs(
                totals[j % 2], t_buf[0 : 2 * rows, span], load_staged_rhs=j // 2 % 2
            )
        p_buf[...] = pltpu.matmul_pop(totals[0]) + pltpu.matmul_pop(totals[1])

    pl.run_scoped(transform, *[pltpu.ACC(o)((2 * rows, MXU), jnp.float32) for o in range(2)])
    product = p_buf[...]
    spectrum = (
        product[0:rows, 0:traces]
        + product[0:rows, traces : 2 * traces]
        + product[rows : 2 * rows, 0:traces]
    ) * (1.0 / math.sqrt(length))
    spectrum = spectrum.astype(jnp.bfloat16)
    for d in range(n):
        send1[d] = spectrum[d * width : (d + 1) * width]

    def copy1(other):
        return pltpu.make_async_remote_copy(
            src_ref=send1.at[other], dst_ref=recv1.at[me],
            send_sem=s1, recv_sem=r1.at[me],
            device_id={"freq": other}, device_id_type=MESH,
        )

    def copy2(other):
        return pltpu.make_async_remote_copy(
            src_ref=send2.at[other], dst_ref=recv2.at[me],
            send_sem=s2, recv_sem=r2.at[upper],
            device_id={"freq": other}, device_id_type=MESH,
        )

    pl.semaphore_wait(barrier, n - 1)

    def start1(i, carry):
        copy1(far(i)).start()
        return carry

    lax.fori_loop(0, n - 1, start1, 0, unroll=n <= 16)

    for copy in small_copies:
        copy.wait()

    def find(t, carry):
        at = jnp.int32(0)
        for k in range(n):
            at = jnp.where(tile_of[k] == t, k, at)
        holder[t] = at
        return carry

    lax.fori_loop(0, n, find, 0)
    spots = [holder[i] for i in range(n)]
    ends = []
    for q in range(per_shot):
        last = rank_of(spots[q])
        for s in range(1, shots):
            late = rank_of(spots[s * per_shot + q])
            last = jnp.where(late > last, late, last)
        ends.append(last)
    ranks = [
        sum([jnp.where(other < end, 1, 0) for other in ends], jnp.int32(0)) for end in ends
    ]
    for j in range(per_shot):
        at = jnp.int32(0)
        picks = [jnp.int32(0)] * shots
        for q, rank in enumerate(ranks):
            at = jnp.where(rank == j, q, at)
            picks = [
                jnp.where(rank == j, spots[s * per_shot + q], pick)
                for s, pick in enumerate(picks)
            ]
        order[j] = at
        for s, pick in enumerate(picks):
            place[s * per_shot + j] = pick

    x_buf[...] = jnp.zeros_like(x_buf)

    for d in range(2):
        pltpu.make_async_copy(op_bufs[d], op_bufs[d], op_sem.at[d]).wait()

    def swap(q, carry):
        for d in range(2):
            swapped[d, q] = op_bufs[d][q].T
        return carry

    lax.fori_loop(0, per_shot, swap, 0, unroll=2)

    def take(i, carry):
        src = seat(i)
        pltpu.make_async_copy(send1.at[src], recv1.at[src], r1.at[src]).wait()
        x_buf[src] = recv1[src].astype(jnp.float32)
        return carry

    first = n - per_shot
    x_buf[me] = send1[me].astype(jnp.float32)
    lax.fori_loop(1, first, take, 0, unroll=n <= 16)
    row = lax.broadcasted_iota(jnp.int32, (turn, traces), 0)
    is_real = row // slots % 2 == 0
    for i in range(2, 2 * slots):
        pltpu.make_async_copy(op_bufs[i], op_bufs[i], op_sem.at[i]).wait()
    tiles = receivers // MXU
    work = [(m, o) for m in reversed(range(slots)) for o in range(tiles)]

    def product(*totals):
        def block(j, carry):
            q = order[j]

            def push(i):
                m, o = work[i]
                span = slice(o * MXU, (o + 1) * MXU)
                if m == 0:
                    tile = jnp.concatenate([swapped[d, q, :, span] for d in range(2)], axis=0)
                else:
                    tile = jnp.concatenate([op_bufs[2 * m + d][q, span] for d in range(2)], axis=1)
                pltpu.matmul_push_rhs(tile, i // 2 % 2, o % 2, transpose=m > 0)

            ready = 4
            for i in range(ready):
                push(i)
            take(first + j, 0)
            for s in range(shots):
                a_buf[j, s * width : (s + 1) * width] = x_buf[place[s * per_shot + j]]
            plain = a_buf[j]
            turned = jnp.where(
                is_real, -pltpu.roll(plain, turn - slots, axis=0), pltpu.roll(plain, slots, axis=0)
            )
            lefts = []
            for m in range(slots):
                pair = jnp.concatenate(
                    [jnp.where(row % slots == m, x, 0.0) for x in (plain, turned)], axis=1
                )
                if height > turn:
                    pair = jnp.concatenate(
                        [pair, jnp.zeros((height - turn, MXU), jnp.float32)], axis=0
                    )
                lefts.append(pair.astype(jnp.bfloat16))
            for i, (m, o) in enumerate(work):
                if ready == 0:
                    push(i)
                pltpu.matmul_acc_lhs(totals[o], lefts[m], load_staged_rhs=i // 2 % 2)
                if ready and i + ready < len(work):
                    push(i + ready)
            return carry

        lax.fori_loop(0, per_shot, block, 0)
        for o, total in enumerate(totals):
            a_pred[:, o * MXU : (o + 1) * MXU] = pltpu.matmul_pop(total)[0:turn]

    height = -(-turn // 16) * 16
    pl.run_scoped(
        product, *[pltpu.ACC(o % 2)((height, MXU), jnp.float32) for o in range(tiles)]
    )
    predicted = a_pred[...]
    row = lax.broadcasted_iota(jnp.int32, (turn, receivers), 0)
    predicted = jnp.where(row % slots < slice_len[me], predicted, 0.0)
    shifted = pltpu.roll(
        jnp.concatenate([predicted, jnp.zeros((turn, traces), jnp.float32)], axis=1), HALO, axis=1
    )
    for t in range(n):
        s, q = t // per_shot, t % per_shot
        pieces[t] = shifted[
            s * width : (s + 1) * width, q * traces : (q + 2) * traces
        ].astype(jnp.bfloat16)

    def start2(i, carry):
        other = i + (i + n - me) // n
        send2[other] = pieces[tile_of[other]]
        copy2(other).start()
        return carry

    lax.fori_loop(0, n - 1, start2, 0, unroll=n <= 16)
    recv2[me] = pieces[tile_of[me]]
    for a in range(TAPS):
        response = lags[0] * filters[0, a, 0:1]
        for c in range(1, 4):
            response = response + lags[c] * filters[0, a, c : c + 1]
        response = jnp.sum(response, axis=1, keepdims=True)
        k_buf[a] = jnp.broadcast_to(response, (2 * rows, traces))
    others = pl.ds(0, n - 1)
    pltpu.make_async_copy(send1.at[others], send1.at[others], s1).wait()
    half = n // 2
    lanes = half * width
    depth = -(-3 * lanes // MXU) * MXU

    def match(side):
        base = pl.multiple_of(side * lanes, lanes)
        z = jnp.concatenate(
            [recv2[side * half + d].astype(jnp.float32) for d in range(half)], axis=0
        )
        direct = jnp.zeros((lanes, traces), jnp.float32)
        cross = jnp.zeros((lanes, traces), jnp.float32)
        for a in range(TAPS):
            moved = (pltpu.roll(z, 2 * traces - a, axis=1) if a else z)[:, 0:traces]
            direct = direct + k_buf[a, pl.ds(base, lanes)] * moved
            cross = cross + k_buf[a, pl.ds(rows + base, lanes)] * moved
        row = lax.broadcasted_iota(jnp.int32, cross.shape, 0)
        matched = direct + jnp.where(
            row // slots % 2 == 0,
            pltpu.roll(cross, lanes - slots, axis=0),
            pltpu.roll(cross, slots, axis=0),
        )
        matched = matched.T
        high = matched.astype(jnp.bfloat16)
        low = (matched - high.astype(jnp.float32)).astype(jnp.bfloat16)
        left = [high, high, low]
        if depth > 3 * lanes:
            left.append(jnp.zeros((traces, depth - 3 * lanes), jnp.bfloat16))
        return base, jnp.concatenate(left, axis=1)

    def subtract(*totals):
        def add(j, base, left, turn_of):
            span = slice(j * MXU, (j + 1) * MXU)
            high = t_buf[pl.ds(base, lanes), span]
            low = t_buf[pl.ds(rows + base, lanes), span]
            right = [high, low, high]
            if depth > 3 * lanes:
                right.append(jnp.zeros((depth - 3 * lanes, MXU), jnp.bfloat16))
            right = jnp.concatenate(right, axis=0)
            for i in range(depth // MXU):
                part = slice(i * MXU, (i + 1) * MXU)
                stage = (turn_of * (depth // MXU) + i) % 2
                pltpu.matmul_push_rhs(right[part], stage, j % 2)
                pltpu.matmul_acc_lhs(totals[j], left[:, part], load_staged_rhs=stage)

        def emit(j):
            span = slice(j * MXU, (j + 1) * MXU)
            out[:, span] = g_buf[:, span] - pltpu.matmul_pop(totals[j])

        count = length // MXU
        near = pl.ds(0, half - 1)
        pltpu.make_async_copy(recv2.at[near], recv2.at[near], r2.at[upper]).wait()
        base, left = match(upper)
        for j in range(count):
            add(j, base, left, j // 2)
        rest = pl.ds(0, half)
        pltpu.make_async_copy(recv2.at[rest], recv2.at[rest], r2.at[1 - upper]).wait()
        base, left = match(1 - upper)
        for j in range(count):
            add(j, base, left, (count + j) // 2)
            if j >= 2:
                emit(j - 2)
        emit(count - 2)
        emit(count - 1)

    pl.run_scoped(
        subtract,
        *[pltpu.ACC(j % 2)((traces, MXU), jnp.float32) for j in range(length // MXU)],
    )
    pltpu.make_async_copy(send2.at[others], send2.at[others], s2).wait()


def local(gathers, operator, filters, tile_of, slice_len):
    n = lax.axis_size("freq")
    traces, length = gathers.shape
    slots, _, receivers, _ = operator.shape
    width = 2 * slots
    rows = n * width
    per_shot = receivers // traces
    turn = n // per_shot * width
    waves = jnp.asarray(wave_table(n, slots, length))
    lags = jnp.asarray(lag_table(n, slots, length, 5 * n // 4))
    hbm = pl.BlockSpec(memory_space=pltpu.HBM)
    taps = filters.transpose(0, 2, 1, 3)
    bf16, f32 = jnp.bfloat16, jnp.float32
    dma = pltpu.SemaphoreType.DMA
    return pl.pallas_call(
        functools.partial(step, n, slots),
        out_shape=jax.ShapeDtypeStruct(gathers.shape, f32),
        in_specs=[hbm] * 7,
        out_specs=pl.BlockSpec(memory_space=pltpu.VMEM),
        scratch_shapes=[
            pltpu.VMEM((traces, length), f32),
            [pltpu.VMEM((per_shot, receivers, traces), bf16)] * (2 * slots),
            pltpu.VMEM((2, per_shot, traces, receivers), bf16),
            pltpu.VMEM((2 * rows, length), bf16),
            pltpu.VMEM((2 * rows, MXU), f32),
            pltpu.VMEM((n, width, traces), bf16),
            pltpu.VMEM((n, width, traces), bf16),
            pltpu.VMEM((n, width, traces), f32),
            pltpu.VMEM((per_shot, turn, traces), f32),
            pltpu.VMEM((turn, receivers), f32),
            pltpu.VMEM((n, width, 2 * traces), bf16),
            pltpu.VMEM((n, width, 2 * traces), bf16),
            pltpu.VMEM((n, width, 2 * traces), bf16),
            pltpu.VMEM((rows // 2, 2 * traces), f32),
            pltpu.VMEM((TAPS, 2 * rows, traces), f32),
            pltpu.SMEM((n,), jnp.int32),
            pltpu.SMEM((n,), jnp.int32),
            pltpu.SMEM((per_shot,), jnp.int32),
            pltpu.VMEM(taps.shape, f32),
            pltpu.VMEM(lags.shape, f32),
            pltpu.SMEM(tile_of.shape, jnp.int32),
            pltpu.SMEM(slice_len.shape, jnp.int32),
            dma((CUTS,)),
            dma((2 * slots,)),
            dma((CUTS,)),
            dma((4,)),
            dma,
            dma((n,)),
            dma,
            dma((2,)),
        ],
        compiler_params=pltpu.CompilerParams(
            collective_id=0, has_side_effects=True, vmem_limit_bytes=48*1024*1024
        ),
    )(*[pltpu.with_memory_space_constraint(x, pltpu.HBM) for x in (gathers, operator, taps, tile_of, slice_len, waves, lags)])


def solution(mesh):
    placed = (
        P(("survey", "freq"), None),
        P(("survey", "freq"), None, None, None),
        P(("survey", "freq"), None, None, None),
        P("survey"),
        P("survey"),
    )
    return jax.shard_map(
        local, mesh=mesh, in_specs=placed, out_specs=P(("survey", "freq"), None), check_vma=False
    )
```

```python
import functools
import math

import jax
import jax.numpy as jnp
import numpy as np
from jax import lax
from jax.experimental import pallas as pl
from jax.experimental.pallas import tpu as pltpu
from jax.sharding import PartitionSpec as P

FIRST = 40
TAPS = 9
HALO = 4
LAGS = 31
MXU = 256
CUTS = 2
MESH = pl.DeviceIdType.MESH


def row_bins(devices, slots):
    row = np.arange(devices * 2 * slots)
    return row // (2 * slots) * slots + row % slots, row // slots % 2


def wave_table(devices, slots, length):
    bins, part = row_bins(devices, slots)
    phase = (FIRST + bins)[:, None] * np.arange(length)[None, :] % length
    angle = 2.0 * math.pi / length * phase
    table = np.where(part[:, None] == 0, np.cos(angle), -np.sin(angle)).astype(np.float32)
    high = table.astype(jnp.bfloat16)
    low = (table - high.astype(np.float32)).astype(jnp.bfloat16)
    return np.concatenate([high, low], axis=0)


def lag_table(devices, slots, length, kept_bins):
    bins, part = row_bins(devices, slots)
    freq = FIRST + bins
    phase = freq[:, None] * (np.arange(LAGS) - LAGS // 2)[None, :] % length
    angle = 2.0 * math.pi / length * phase
    cosine, sine = np.cos(angle), np.sin(angle)
    weight = (freq / (FIRST + devices * slots))[:, None]
    real = np.stack([cosine, sine, -weight * sine, weight * cosine])
    imag = np.stack([sine, -cosine, weight * cosine, weight * sine])
    imag = np.where(part[None, :, None] == 0, imag, -imag)
    scale = math.sqrt(2.0 / kept_bins)
    return (np.concatenate([real, imag], axis=1) * scale).astype(np.float32)


def step(
    n, slots, gathers, operator, filters_hbm, tile_hbm, len_hbm, waves, lags_hbm, out,
    g_buf, op_bufs, swapped, t_buf, p_buf, send1, recv1, x_buf, a_buf, a_pred, pieces, send2, recv2,
    z_buf, k_buf, holder, place, order, filters, lags, tile_of, slice_len,
    g_sem, op_sem, t_sem, small_sem, s1, r1, s2, r2,
):
    me = lax.axis_index("freq")
    traces, length = g_buf.shape
    receivers = op_bufs[0].shape[1]
    width = 2 * slots
    rows = n * width
    per_shot = receivers // traces
    shots = n // per_shot
    turn = shots * width

    upper = me // (n // 2)
    reach = upper * (n - 1 - me) + (1 - upper) * me

    def seat(i):
        inside = (2 * reach - i + n) // n
        close = me + (1 - 2 * (i % 2)) * ((i + 1) // 2)
        return inside * close + (1 - inside) * (upper * (n - 1 - i) + (1 - upper) * i)

    def rank_of(k):
        ahead = k - me
        close = jnp.where(ahead > 0, 2 * ahead, jnp.where(ahead < 0, -2 * ahead - 1, 0))
        return jnp.where(close > 2 * reach, upper * (n - 1 - k) + (1 - upper) * k, close)

    def far(i):
        return seat(n - 1 - i)

    barrier = pltpu.get_barrier_semaphore()

    def greet(i, carry):
        pl.semaphore_signal(
            barrier, inc=1, device_id={"freq": far(i)}, device_id_type=MESH
        )
        return carry

    lax.fori_loop(0, n - 1, greet, 0, unroll=n <= 16)

    piece = length // CUTS
    g_copies, t_copies = [], []
    for j in range(CUTS):
        span = pl.ds(j * piece, piece)
        copy = pltpu.make_async_copy(gathers.at[:, span], g_buf.at[:, span], g_sem.at[j])
        copy.start()
        g_copies.append(copy)
        copy = pltpu.make_async_copy(
            waves.at[:, span], t_buf.at[:, span], t_sem.at[j]
        )
        copy.start()
        t_copies.append(copy)
    small_copies = []
    for i, (src, dst) in enumerate(
        ((filters_hbm, filters), (lags_hbm, lags), (tile_hbm, tile_of), (len_hbm, slice_len))
    ):
        copy = pltpu.make_async_copy(src, dst, small_sem.at[i])
        copy.start()
        small_copies.append(copy)
    for m in range(slots):
        for d in range(2):
            for q in range(per_shot):
                pltpu.make_async_copy(
                    operator.at[m, d, :, pl.ds(q * traces, traces)],
                    op_bufs[2 * m + d].at[q], op_sem.at[2 * m + d],
                ).start(priority=1)


    def transform(*totals):
        for j in range(length // MXU):
            span = slice(j * MXU, (j + 1) * MXU)
            if j * MXU % piece == 0:
                g_copies[j * MXU // piece].wait()
                t_copies[j * MXU // piece].wait()
            data = g_buf[:, span]
            high = data.astype(jnp.bfloat16)
            low = (data - high.astype(jnp.float32)).astype(jnp.bfloat16)
            pairs = jnp.concatenate([high, low], axis=0)
            pltpu.matmul_push_rhs(pairs, j // 2 % 2, j % 2, transpose=True)
            pltpu.matmul_acc_lhs(
                totals[j % 2], t_buf[0 : 2 * rows, span], load_staged_rhs=j // 2 % 2
            )
        p_buf[...] = pltpu.matmul_pop(totals[0]) + pltpu.matmul_pop(totals[1])

    pl.run_scoped(transform, *[pltpu.ACC(o)((2 * rows, MXU), jnp.float32) for o in range(2)])
    product = p_buf[...]
    spectrum = (
        product[0:rows, 0:traces]
        + product[0:rows, traces : 2 * traces]
        + product[rows : 2 * rows, 0:traces]
    ) * (1.0 / math.sqrt(length))
    spectrum = spectrum.astype(jnp.bfloat16)
    for d in range(n):
        send1[d] = spectrum[d * width : (d + 1) * width]

    def copy1(other):
        return pltpu.make_async_remote_copy(
            src_ref=send1.at[other], dst_ref=recv1.at[me],
            send_sem=s1, recv_sem=r1.at[me],
            device_id={"freq": other}, device_id_type=MESH,
        )

    def copy2(other):
        return pltpu.make_async_remote_copy(
            src_ref=send2.at[other], dst_ref=recv2.at[me],
            send_sem=s2, recv_sem=r2.at[upper],
            device_id={"freq": other}, device_id_type=MESH,
        )

    pl.semaphore_wait(barrier, n - 1)

    def start1(i, carry):
        copy1(far(i)).start()
        return carry

    lax.fori_loop(0, n - 1, start1, 0, unroll=n <= 16)

    for copy in small_copies:
        copy.wait()

    def find(t, carry):
        at = jnp.int32(0)
        for k in range(n):
            at = jnp.where(tile_of[k] == t, k, at)
        holder[t] = at
        return carry

    lax.fori_loop(0, n, find, 0)
    spots = [holder[i] for i in range(n)]
    ends = []
    for q in range(per_shot):
        last = rank_of(spots[q])
        for s in range(1, shots):
            late = rank_of(spots[s * per_shot + q])
            last = jnp.where(late > last, late, last)
        ends.append(last)
    ranks = [
        sum([jnp.where(other < end, 1, 0) for other in ends], jnp.int32(0)) for end in ends
    ]
    for j in range(per_shot):
        at = jnp.int32(0)
        picks = [jnp.int32(0)] * shots
        for q, rank in enumerate(ranks):
            at = jnp.where(rank == j, q, at)
            picks = [
                jnp.where(rank == j, spots[s * per_shot + q], pick)
                for s, pick in enumerate(picks)
            ]
        order[j] = at
        for s, pick in enumerate(picks):
            place[s * per_shot + j] = pick

    x_buf[...] = jnp.zeros_like(x_buf)

    for d in range(2):
        pltpu.make_async_copy(op_bufs[d], op_bufs[d], op_sem.at[d]).wait()

    def swap(q, carry):
        for d in range(2):
            swapped[d, q] = op_bufs[d][q].T
        return carry

    lax.fori_loop(0, per_shot, swap, 0, unroll=2)

    def take(i, carry):
        src = seat(i)
        pltpu.make_async_copy(send1.at[src], recv1.at[src], r1.at[src]).wait()
        x_buf[src] = recv1[src].astype(jnp.float32)
        return carry

    first = n - per_shot
    x_buf[me] = send1[me].astype(jnp.float32)
    lax.fori_loop(1, first, take, 0, unroll=n <= 16)
    row = lax.broadcasted_iota(jnp.int32, (turn, traces), 0)
    is_real = row // slots % 2 == 0
    for i in range(2, 2 * slots):
        pltpu.make_async_copy(op_bufs[i], op_bufs[i], op_sem.at[i]).wait()
    tiles = receivers // MXU
    work = [(m, o) for m in reversed(range(slots)) for o in range(tiles)]

    def product(*totals):
        def block(j, carry):
            q = order[j]

            def push(i):
                m, o = work[i]
                span = slice(o * MXU, (o + 1) * MXU)
                if m == 0:
                    tile = jnp.concatenate([swapped[d, q, :, span] for d in range(2)], axis=0)
                else:
                    tile = jnp.concatenate([op_bufs[2 * m + d][q, span] for d in range(2)], axis=1)
                pltpu.matmul_push_rhs(tile, i // 2 % 2, o % 2, transpose=m > 0)

            ready = 4
            for i in range(ready):
                push(i)
            take(first + j, 0)
            for s in range(shots):
                a_buf[j, s * width : (s + 1) * width] = x_buf[place[s * per_shot + j]]
            plain = a_buf[j]
            turned = jnp.where(
                is_real, -pltpu.roll(plain, turn - slots, axis=0), pltpu.roll(plain, slots, axis=0)
            )
            lefts = []
            for m in range(slots):
                pair = jnp.concatenate(
                    [jnp.where(row % slots == m, x, 0.0) for x in (plain, turned)], axis=1
                )
                if height > turn:
                    pair = jnp.concatenate(
                        [pair, jnp.zeros((height - turn, MXU), jnp.float32)], axis=0
                    )
                lefts.append(pair.astype(jnp.bfloat16))
            for i, (m, o) in enumerate(work):
                if ready == 0:
                    push(i)
                pltpu.matmul_acc_lhs(totals[o], lefts[m], load_staged_rhs=i // 2 % 2)
                if ready and i + ready < len(work):
                    push(i + ready)
            return carry

        lax.fori_loop(0, per_shot, block, 0)
        for o, total in enumerate(totals):
            a_pred[:, o * MXU : (o + 1) * MXU] = pltpu.matmul_pop(total)[0:turn]

    height = -(-turn // 16) * 16
    pl.run_scoped(
        product, *[pltpu.ACC(o % 2)((height, MXU), jnp.float32) for o in range(tiles)]
    )
    predicted = a_pred[...]
    row = lax.broadcasted_iota(jnp.int32, (turn, receivers), 0)
    predicted = jnp.where(row % slots < slice_len[me], predicted, 0.0)
    shifted = pltpu.roll(
        jnp.concatenate([predicted, jnp.zeros((turn, traces), jnp.float32)], axis=1), HALO, axis=1
    )
    for t in range(n):
        s, q = t // per_shot, t % per_shot
        pieces[t] = shifted[
            s * width : (s + 1) * width, q * traces : (q + 2) * traces
        ].astype(jnp.bfloat16)

    def start2(i, carry):
        other = far(i)
        send2[other] = pieces[tile_of[other]]
        copy2(other).start()
        return carry

    lax.fori_loop(0, n - 1, start2, 0, unroll=n <= 16)
    recv2[me] = pieces[tile_of[me]]
    for a in range(TAPS):
        response = lags[0] * filters[0, a, 0:1]
        for c in range(1, 4):
            response = response + lags[c] * filters[0, a, c : c + 1]
        response = jnp.sum(response, axis=1, keepdims=True)
        k_buf[a] = jnp.broadcast_to(response, (2 * rows, traces))
    others = pl.ds(0, n - 1)
    pltpu.make_async_copy(send1.at[others], send1.at[others], s1).wait()
    half = n // 2
    lanes = half * width
    depth = -(-3 * lanes // MXU) * MXU

    def match(side):
        base = pl.multiple_of(side * lanes, lanes)
        z = jnp.concatenate(
            [recv2[side * half + d].astype(jnp.float32) for d in range(half)], axis=0
        )
        direct = jnp.zeros((lanes, traces), jnp.float32)
        cross = jnp.zeros((lanes, traces), jnp.float32)
        for a in range(TAPS):
            moved = (pltpu.roll(z, 2 * traces - a, axis=1) if a else z)[:, 0:traces]
            direct = direct + k_buf[a, pl.ds(base, lanes)] * moved
            cross = cross + k_buf[a, pl.ds(rows + base, lanes)] * moved
        row = lax.broadcasted_iota(jnp.int32, cross.shape, 0)
        matched = direct + jnp.where(
            row // slots % 2 == 0,
            pltpu.roll(cross, lanes - slots, axis=0),
            pltpu.roll(cross, slots, axis=0),
        )
        matched = matched.T
        high = matched.astype(jnp.bfloat16)
        low = (matched - high.astype(jnp.float32)).astype(jnp.bfloat16)
        left = [high, high, low]
        if depth > 3 * lanes:
            left.append(jnp.zeros((traces, depth - 3 * lanes), jnp.bfloat16))
        return base, jnp.concatenate(left, axis=1)

    def subtract(*totals):
        def add(j, base, left, turn_of):
            span = slice(j * MXU, (j + 1) * MXU)
            high = t_buf[pl.ds(base, lanes), span]
            low = t_buf[pl.ds(rows + base, lanes), span]
            right = [high, low, high]
            if depth > 3 * lanes:
                right.append(jnp.zeros((depth - 3 * lanes, MXU), jnp.bfloat16))
            right = jnp.concatenate(right, axis=0)
            for i in range(depth // MXU):
                part = slice(i * MXU, (i + 1) * MXU)
                stage = (turn_of * (depth // MXU) + i) % 2
                pltpu.matmul_push_rhs(right[part], stage, j % 2)
                pltpu.matmul_acc_lhs(totals[j], left[:, part], load_staged_rhs=stage)

        def emit(j):
            span = slice(j * MXU, (j + 1) * MXU)
            out[:, span] = g_buf[:, span] - pltpu.matmul_pop(totals[j])

        count = length // MXU
        near = pl.ds(0, half - 1)
        pltpu.make_async_copy(recv2.at[near], recv2.at[near], r2.at[upper]).wait()
        base, left = match(upper)
        for j in range(count):
            add(j, base, left, j // 2)
        rest = pl.ds(0, half)
        pltpu.make_async_copy(recv2.at[rest], recv2.at[rest], r2.at[1 - upper]).wait()
        base, left = match(1 - upper)
        for j in range(count):
            add(j, base, left, (count + j) // 2)
            if j >= 2:
                emit(j - 2)
        emit(count - 2)
        emit(count - 1)

    pl.run_scoped(
        subtract,
        *[pltpu.ACC(j % 2)((traces, MXU), jnp.float32) for j in range(length // MXU)],
    )
    pltpu.make_async_copy(send2.at[others], send2.at[others], s2).wait()


def local(gathers, operator, filters, tile_of, slice_len):
    n = lax.axis_size("freq")
    traces, length = gathers.shape
    slots, _, receivers, _ = operator.shape
    width = 2 * slots
    rows = n * width
    per_shot = receivers // traces
    turn = n // per_shot * width
    waves = jnp.asarray(wave_table(n, slots, length))
    lags = jnp.asarray(lag_table(n, slots, length, 5 * n // 4))
    hbm = pl.BlockSpec(memory_space=pltpu.HBM)
    taps = filters.transpose(0, 2, 1, 3)
    bf16, f32 = jnp.bfloat16, jnp.float32
    dma = pltpu.SemaphoreType.DMA
    return pl.pallas_call(
        functools.partial(step, n, slots),
        out_shape=jax.ShapeDtypeStruct(gathers.shape, f32),
        in_specs=[hbm] * 7,
        out_specs=pl.BlockSpec(memory_space=pltpu.VMEM),
        scratch_shapes=[
            pltpu.VMEM((traces, length), f32),
            [pltpu.VMEM((per_shot, receivers, traces), bf16)] * (2 * slots),
            pltpu.VMEM((2, per_shot, traces, receivers), bf16),
            pltpu.VMEM((2 * rows, length), bf16),
            pltpu.VMEM((2 * rows, MXU), f32),
            pltpu.VMEM((n, width, traces), bf16),
            pltpu.VMEM((n, width, traces), bf16),
            pltpu.VMEM((n, width, traces), f32),
            pltpu.VMEM((per_shot, turn, traces), f32),
            pltpu.VMEM((turn, receivers), f32),
            pltpu.VMEM((n, width, 2 * traces), bf16),
            pltpu.VMEM((n, width, 2 * traces), bf16),
            pltpu.VMEM((n, width, 2 * traces), bf16),
            pltpu.VMEM((rows // 2, 2 * traces), f32),
            pltpu.VMEM((TAPS, 2 * rows, traces), f32),
            pltpu.SMEM((n,), jnp.int32),
            pltpu.SMEM((n,), jnp.int32),
            pltpu.SMEM((per_shot,), jnp.int32),
            pltpu.VMEM(taps.shape, f32),
            pltpu.VMEM(lags.shape, f32),
            pltpu.SMEM(tile_of.shape, jnp.int32),
            pltpu.SMEM(slice_len.shape, jnp.int32),
            dma((CUTS,)),
            dma((2 * slots,)),
            dma((CUTS,)),
            dma((4,)),
            dma,
            dma((n,)),
            dma,
            dma((2,)),
        ],
        compiler_params=pltpu.CompilerParams(
            collective_id=0, has_side_effects=True, vmem_limit_bytes=48*1024*1024
        ),
    )(*[pltpu.with_memory_space_constraint(x, pltpu.HBM) for x in (gathers, operator, taps, tile_of, slice_len, waves, lags)])


def solution(mesh):
    placed = (
        P(("survey", "freq"), None),
        P(("survey", "freq"), None, None, None),
        P(("survey", "freq"), None, None, None),
        P("survey"),
        P("survey"),
    )
    return jax.shard_map(
        local, mesh=mesh, in_specs=placed, out_specs=P(("survey", "freq"), None), check_vma=False
    )
```

```python
import functools
import math

import jax
import jax.numpy as jnp
import numpy as np
from jax import lax
from jax.experimental import pallas as pl
from jax.experimental.pallas import tpu as pltpu
from jax.sharding import PartitionSpec as P

FIRST = 40
TAPS = 9
HALO = 4
LAGS = 31
MXU = 256
CUTS = 2
MESH = pl.DeviceIdType.MESH


def row_bins(devices, slots):
    row = np.arange(devices * 2 * slots)
    return row // (2 * slots) * slots + row % slots, row // slots % 2


def wave_table(devices, slots, length):
    bins, part = row_bins(devices, slots)
    phase = (FIRST + bins)[:, None] * np.arange(length)[None, :] % length
    angle = 2.0 * math.pi / length * phase
    table = np.where(part[:, None] == 0, np.cos(angle), -np.sin(angle)).astype(np.float32)
    high = table.astype(jnp.bfloat16)
    low = (table - high.astype(np.float32)).astype(jnp.bfloat16)
    return np.concatenate([high, low], axis=0)


def lag_table(devices, slots, length, kept_bins):
    bins, part = row_bins(devices, slots)
    freq = FIRST + bins
    phase = freq[:, None] * (np.arange(LAGS) - LAGS // 2)[None, :] % length
    angle = 2.0 * math.pi / length * phase
    cosine, sine = np.cos(angle), np.sin(angle)
    weight = (freq / (FIRST + devices * slots))[:, None]
    real = np.stack([cosine, sine, -weight * sine, weight * cosine])
    imag = np.stack([sine, -cosine, weight * cosine, weight * sine])
    imag = np.where(part[None, :, None] == 0, imag, -imag)
    scale = math.sqrt(2.0 / kept_bins)
    return (np.concatenate([real, imag], axis=1) * scale).astype(np.float32)


def step(
    n, slots, gathers, operator, filters_hbm, tile_hbm, len_hbm, waves, lags_hbm, out,
    g_buf, op_bufs, swapped, t_buf, p_buf, send1, recv1, x_buf, a_buf, pieces, send2, recv2,
    z_buf, k_buf, holder, place, order, filters, lags, tile_of, slice_len,
    g_sem, op_sem, t_sem, small_sem, s1, r1, s2, r2,
):
    me = lax.axis_index("freq")
    traces, length = g_buf.shape
    receivers = op_bufs[0].shape[1]
    width = 2 * slots
    rows = n * width
    per_shot = receivers // traces
    shots = n // per_shot
    turn = shots * width

    upper = me // (n // 2)
    reach = upper * (n - 1 - me) + (1 - upper) * me

    def seat(i):
        inside = (2 * reach - i + n) // n
        close = me + (1 - 2 * (i % 2)) * ((i + 1) // 2)
        return inside * close + (1 - inside) * (upper * (n - 1 - i) + (1 - upper) * i)

    def rank_of(k):
        ahead = k - me
        close = jnp.where(ahead > 0, 2 * ahead, jnp.where(ahead < 0, -2 * ahead - 1, 0))
        return jnp.where(close > 2 * reach, upper * (n - 1 - k) + (1 - upper) * k, close)

    def far(i):
        return seat(n - 1 - i)

    barrier = pltpu.get_barrier_semaphore()

    def greet(i, carry):
        pl.semaphore_signal(
            barrier, inc=1, device_id={"freq": far(i)}, device_id_type=MESH
        )
        return carry

    lax.fori_loop(0, n - 1, greet, 0, unroll=n <= 16)

    piece = length // CUTS
    g_copies, t_copies = [], []
    for j in range(CUTS):
        span = pl.ds(j * piece, piece)
        copy = pltpu.make_async_copy(gathers.at[:, span], g_buf.at[:, span], g_sem.at[j])
        copy.start()
        g_copies.append(copy)
        copy = pltpu.make_async_copy(
            waves.at[:, span], t_buf.at[:, span], t_sem.at[j]
        )
        copy.start()
        t_copies.append(copy)
    small_copies = []
    for i, (src, dst) in enumerate(
        ((filters_hbm, filters), (lags_hbm, lags), (tile_hbm, tile_of), (len_hbm, slice_len))
    ):
        copy = pltpu.make_async_copy(src, dst, small_sem.at[i])
        copy.start()
        small_copies.append(copy)
    for m in range(slots):
        for d in range(2):
            for q in range(per_shot):
                pltpu.make_async_copy(
                    operator.at[m, d, :, pl.ds(q * traces, traces)],
                    op_bufs[2 * m + d].at[q], op_sem.at[2 * m + d],
                ).start(priority=1)


    def transform(*totals):
        for j in range(length // MXU):
            span = slice(j * MXU, (j + 1) * MXU)
            if j * MXU % piece == 0:
                g_copies[j * MXU // piece].wait()
                t_copies[j * MXU // piece].wait()
            data = g_buf[:, span]
            high = data.astype(jnp.bfloat16)
            low = (data - high.astype(jnp.float32)).astype(jnp.bfloat16)
            pairs = jnp.concatenate([high, low], axis=0)
            pltpu.matmul_push_rhs(pairs, j // 2 % 2, j % 2, transpose=True)
            pltpu.matmul_acc_lhs(
                totals[j % 2], t_buf[0 : 2 * rows, span], load_staged_rhs=j // 2 % 2
            )
        p_buf[...] = pltpu.matmul_pop(totals[0]) + pltpu.matmul_pop(totals[1])

    pl.run_scoped(transform, *[pltpu.ACC(o)((2 * rows, MXU), jnp.float32) for o in range(2)])
    product = p_buf[...]
    spectrum = (
        product[0:rows, 0:traces]
        + product[0:rows, traces : 2 * traces]
        + product[rows : 2 * rows, 0:traces]
    ) * (1.0 / math.sqrt(length))
    spectrum = spectrum.astype(jnp.bfloat16)
    for d in range(n):
        send1[d] = spectrum[d * width : (d + 1) * width]

    def copy1(other):
        return pltpu.make_async_remote_copy(
            src_ref=send1.at[other], dst_ref=recv1.at[me],
            send_sem=s1, recv_sem=r1.at[me],
            device_id={"freq": other}, device_id_type=MESH,
        )

    def copy2(other):
        return pltpu.make_async_remote_copy(
            src_ref=send2.at[other], dst_ref=recv2.at[me],
            send_sem=s2, recv_sem=r2.at[upper],
            device_id={"freq": other}, device_id_type=MESH,
        )

    pl.semaphore_wait(barrier, n - 1)

    def start1(i, carry):
        copy1(far(i)).start()
        return carry

    lax.fori_loop(0, n - 1, start1, 0, unroll=n <= 16)

    for copy in small_copies:
        copy.wait()

    def find(t, carry):
        at = jnp.int32(0)
        for k in range(n):
            at = jnp.where(tile_of[k] == t, k, at)
        holder[t] = at
        return carry

    lax.fori_loop(0, n, find, 0)
    spots = [holder[i] for i in range(n)]
    ends = []
    for q in range(per_shot):
        last = rank_of(spots[q])
        for s in range(1, shots):
            late = rank_of(spots[s * per_shot + q])
            last = jnp.where(late > last, late, last)
        ends.append(last)
    ranks = [
        sum([jnp.where(other < end, 1, 0) for other in ends], jnp.int32(0)) for end in ends
    ]
    for j in range(per_shot):
        at = jnp.int32(0)
        picks = [jnp.int32(0)] * shots
        for q, rank in enumerate(ranks):
            at = jnp.where(rank == j, q, at)
            picks = [
                jnp.where(rank == j, spots[s * per_shot + q], pick)
                for s, pick in enumerate(picks)
            ]
        order[j] = at
        for s, pick in enumerate(picks):
            place[s * per_shot + j] = pick

    x_buf[...] = jnp.zeros_like(x_buf)

    for d in range(2):
        pltpu.make_async_copy(op_bufs[d], op_bufs[d], op_sem.at[d]).wait()

    def swap(q, carry):
        for d in range(2):
            swapped[d, q] = op_bufs[d][q].T
        return carry

    lax.fori_loop(0, per_shot, swap, 0, unroll=2)

    def take(i, carry):
        src = seat(i)
        pltpu.make_async_copy(send1.at[src], recv1.at[src], r1.at[src]).wait()
        x_buf[src] = recv1[src].astype(jnp.float32)
        return carry

    first = n - per_shot
    x_buf[me] = send1[me].astype(jnp.float32)
    lax.fori_loop(1, first, take, 0, unroll=n <= 16)
    row = lax.broadcasted_iota(jnp.int32, (turn, traces), 0)
    is_real = row // slots % 2 == 0
    for i in range(2, 2 * slots):
        pltpu.make_async_copy(op_bufs[i], op_bufs[i], op_sem.at[i]).wait()
    tiles = receivers // MXU
    work = [(m, o) for m in reversed(range(slots)) for o in range(tiles)]

    def product(*totals):
        def block(j, carry):
            q = order[j]

            def push(i):
                m, o = work[i]
                span = slice(o * MXU, (o + 1) * MXU)
                if m == 0:
                    tile = jnp.concatenate([swapped[d, q, :, span] for d in range(2)], axis=0)
                else:
                    tile = jnp.concatenate([op_bufs[2 * m + d][q, span] for d in range(2)], axis=1)
                pltpu.matmul_push_rhs(tile, i // 2 % 2, o % 2, transpose=m > 0)

            ready = 4
            for i in range(ready):
                push(i)
            take(first + j, 0)
            for s in range(shots):
                a_buf[j, s * width : (s + 1) * width] = x_buf[place[s * per_shot + j]]
            plain = a_buf[j]
            turned = jnp.where(
                is_real, -pltpu.roll(plain, turn - slots, axis=0), pltpu.roll(plain, slots, axis=0)
            )
            lefts = []
            for m in range(slots):
                pair = jnp.concatenate(
                    [jnp.where(row % slots == m, x, 0.0) for x in (plain, turned)], axis=1
                )
                if height > turn:
                    pair = jnp.concatenate(
                        [pair, jnp.zeros((height - turn, MXU), jnp.float32)], axis=0
                    )
                lefts.append(pair.astype(jnp.bfloat16))
            for i, (m, o) in enumerate(work):
                if ready == 0:
                    push(i)
                pltpu.matmul_acc_lhs(totals[o], lefts[m], load_staged_rhs=i // 2 % 2)
                if ready and i + ready < len(work):
                    push(i + ready)
            return carry

        lax.fori_loop(0, per_shot, block, 0)
        return jnp.concatenate([pltpu.matmul_pop(total)[0:turn] for total in totals], axis=1)

    height = -(-turn // 16) * 16
    predicted = pl.run_scoped(
        product, *[pltpu.ACC(o % 2)((height, MXU), jnp.float32) for o in range(tiles)]
    )
    row = lax.broadcasted_iota(jnp.int32, (turn, receivers), 0)
    predicted = jnp.where(row % slots < slice_len[me], predicted, 0.0)
    shifted = pltpu.roll(
        jnp.concatenate([predicted, jnp.zeros((turn, traces), jnp.float32)], axis=1), HALO, axis=1
    )
    for t in range(n):
        s, q = t // per_shot, t % per_shot
        pieces[t] = shifted[
            s * width : (s + 1) * width, q * traces : (q + 2) * traces
        ].astype(jnp.bfloat16)

    def start2(i, carry):
        other = far(i)
        send2[other] = pieces[tile_of[other]]
        copy2(other).start()
        return carry

    lax.fori_loop(0, n - 1, start2, 0, unroll=n <= 16)
    recv2[me] = pieces[tile_of[me]]
    for a in range(TAPS):
        response = lags[0] * filters[0, a, 0:1]
        for c in range(1, 4):
            response = response + lags[c] * filters[0, a, c : c + 1]
        response = jnp.sum(response, axis=1, keepdims=True)
        k_buf[a] = jnp.broadcast_to(response, (2 * rows, traces))
    others = pl.ds(0, n - 1)
    pltpu.make_async_copy(send1.at[others], send1.at[others], s1).wait()
    half = n // 2
    lanes = half * width
    depth = -(-3 * lanes // MXU) * MXU

    def match(side):
        base = pl.multiple_of(side * lanes, lanes)
        z = jnp.concatenate(
            [recv2[side * half + d].astype(jnp.float32) for d in range(half)], axis=0
        )
        direct = jnp.zeros((lanes, traces), jnp.float32)
        cross = jnp.zeros((lanes, traces), jnp.float32)
        for a in range(TAPS):
            moved = (pltpu.roll(z, 2 * traces - a, axis=1) if a else z)[:, 0:traces]
            direct = direct + k_buf[a, pl.ds(base, lanes)] * moved
            cross = cross + k_buf[a, pl.ds(rows + base, lanes)] * moved
        row = lax.broadcasted_iota(jnp.int32, cross.shape, 0)
        matched = direct + jnp.where(
            row // slots % 2 == 0,
            pltpu.roll(cross, lanes - slots, axis=0),
            pltpu.roll(cross, slots, axis=0),
        )
        matched = matched.T
        high = matched.astype(jnp.bfloat16)
        low = (matched - high.astype(jnp.float32)).astype(jnp.bfloat16)
        left = [high, high, low]
        if depth > 3 * lanes:
            left.append(jnp.zeros((traces, depth - 3 * lanes), jnp.bfloat16))
        return base, jnp.concatenate(left, axis=1)

    def subtract(*totals):
        def add(j, base, left, turn_of):
            span = slice(j * MXU, (j + 1) * MXU)
            high = t_buf[pl.ds(base, lanes), span]
            low = t_buf[pl.ds(rows + base, lanes), span]
            right = [high, low, high]
            if depth > 3 * lanes:
                right.append(jnp.zeros((depth - 3 * lanes, MXU), jnp.bfloat16))
            right = jnp.concatenate(right, axis=0)
            for i in range(depth // MXU):
                part = slice(i * MXU, (i + 1) * MXU)
                stage = (turn_of * (depth // MXU) + i) % 2
                pltpu.matmul_push_rhs(right[part], stage, j % 2)
                pltpu.matmul_acc_lhs(totals[j], left[:, part], load_staged_rhs=stage)

        def emit(j):
            span = slice(j * MXU, (j + 1) * MXU)
            out[:, span] = g_buf[:, span] - pltpu.matmul_pop(totals[j])

        count = length // MXU
        near = pl.ds(0, half - 1)
        pltpu.make_async_copy(recv2.at[near], recv2.at[near], r2.at[upper]).wait()
        base, left = match(upper)
        for j in range(count):
            add(j, base, left, j // 2)
        rest = pl.ds(0, half)
        pltpu.make_async_copy(recv2.at[rest], recv2.at[rest], r2.at[1 - upper]).wait()
        base, left = match(1 - upper)
        for j in range(count):
            add(j, base, left, (count + j) // 2)
            if j >= 2:
                emit(j - 2)
        emit(count - 2)
        emit(count - 1)

    pl.run_scoped(
        subtract,
        *[pltpu.ACC(j % 2)((traces, MXU), jnp.float32) for j in range(length // MXU)],
    )
    pltpu.make_async_copy(send2.at[others], send2.at[others], s2).wait()


def local(gathers, operator, filters, tile_of, slice_len):
    n = lax.axis_size("freq")
    traces, length = gathers.shape
    slots, _, receivers, _ = operator.shape
    width = 2 * slots
    rows = n * width
    per_shot = receivers // traces
    turn = n // per_shot * width
    waves = jnp.asarray(wave_table(n, slots, length))
    lags = jnp.asarray(lag_table(n, slots, length, 5 * n // 4))
    hbm = pl.BlockSpec(memory_space=pltpu.HBM)
    taps = filters.transpose(0, 2, 1, 3)
    bf16, f32 = jnp.bfloat16, jnp.float32
    dma = pltpu.SemaphoreType.DMA
    return pl.pallas_call(
        functools.partial(step, n, slots),
        out_shape=jax.ShapeDtypeStruct(gathers.shape, f32),
        in_specs=[hbm] * 7,
        out_specs=pl.BlockSpec(memory_space=pltpu.VMEM),
        scratch_shapes=[
            pltpu.VMEM((traces, length), f32),
            [pltpu.VMEM((per_shot, receivers, traces), bf16)] * (2 * slots),
            pltpu.VMEM((2, per_shot, traces, receivers), bf16),
            pltpu.VMEM((2 * rows, length), bf16),
            pltpu.VMEM((2 * rows, MXU), f32),
            pltpu.VMEM((n, width, traces), bf16),
            pltpu.VMEM((n, width, traces), bf16),
            pltpu.VMEM((n, width, traces), f32),
            pltpu.VMEM((per_shot, turn, traces), f32),
            pltpu.VMEM((n, width, 2 * traces), bf16),
            pltpu.VMEM((n, width, 2 * traces), bf16),
            pltpu.VMEM((n, width, 2 * traces), bf16),
            pltpu.VMEM((rows // 2, 2 * traces), f32),
            pltpu.VMEM((TAPS, 2 * rows, traces), f32),
            pltpu.SMEM((n,), jnp.int32),
            pltpu.SMEM((n,), jnp.int32),
            pltpu.SMEM((per_shot,), jnp.int32),
            pltpu.VMEM(taps.shape, f32),
            pltpu.VMEM(lags.shape, f32),
            pltpu.SMEM(tile_of.shape, jnp.int32),
            pltpu.SMEM(slice_len.shape, jnp.int32),
            dma((CUTS,)),
            dma((2 * slots,)),
            dma((CUTS,)),
            dma((4,)),
            dma,
            dma((n,)),
            dma,
            dma((2,)),
        ],
        compiler_params=pltpu.CompilerParams(
            collective_id=0, has_side_effects=True, vmem_limit_bytes=48*1024*1024
        ),
    )(*[pltpu.with_memory_space_constraint(x, pltpu.HBM) for x in (gathers, operator, taps, tile_of, slice_len, waves, lags)])


def solution(mesh):
    placed = (
        P(("survey", "freq"), None),
        P(("survey", "freq"), None, None, None),
        P(("survey", "freq"), None, None, None),
        P("survey"),
        P("survey"),
    )
    return jax.shard_map(
        local, mesh=mesh, in_specs=placed, out_specs=P(("survey", "freq"), None), check_vma=False
    )
```
